32 devices in a mesh: dp: 4 (over y, x), expert: 8 (over z, core).
Axes of the slice: x: 2, y: 2, z: 4, core: 2. Of those that a mesh axis runs over, the one named last changes fastest.
Arguments:
- item_feats: bfloat16 [8, 2048, 256], P('expert', 'dp'), may hold values from -6 to 6
- expert_ids: int32 [8, 2048, 1], P('expert', 'dp'), may hold values from 0 to 31; in each aligned block of 512 rows (0 to 511, 512 to 1023, ..., all dimensions but the last counted through in order) at most 32 rows name the same one
- weight_in: bfloat16 [32, 256, 1024], P('expert'), may hold values from -0.375 to 0.375
- weight_out: bfloat16 [32, 1024, 256], P('expert'), may hold values from -0.1875 to 0.1875
- queries: bfloat16 [8, 2048, 256], P('expert', 'dp'), may hold values from -150 to 150
- query_weight: float32 [8, 2048], P('expert', 'dp'), may hold values from 0.25 to 2
- positives: int32 [8, 2048], P('expert', 'dp'), may hold values from 0 to 2047
- sample_counts: int32 [8, 2048], P('expert'), may hold values from 1 to 4095
Outputs:
- query_loss: float32 [8, 2048], P('expert', 'dp')
- grad_queries: float32 [8, 2048, 256], P('expert', 'dp')
- grad_items: float32 [8, 2048, 256], P('expert', 'dp')
- grad_weight_in: float32 [256, 32, 1024], P('dp', 'expert')
- grad_weight_out: float32 [1024, 32, 256], P('dp', 'expert')
The draws below stay inside these ranges and needn't reach their ends.
Inputs may be any that keep to these rules, and one draw needn't show every extreme that they name: `expert_ids`: the 512 items of one device name each expert at most 32 times.
All inputs are finite; a program needn't handle non-finite values.
Results may differ from the reference program's by a relative error of at most 0.023.
The reference program's roundings to bfloat16 on the way count: a program that leaves them out, or rounds other values in their place, can miss the bound.
Values may be sent and summed in bfloat16 or wider, within the bound.
No kernel may reach another device: no remote copies, remote signals or barrier semaphores. Data moves between devices by JAX's collectives and lax.ppermute only.
A program may use at most 128 MiB of HBM per device.

```python
import math
import jax
import jax.numpy as jnp
import numpy as np
from jax import lax

D = 256
FF = 1024
ITEM_DEV = 512
EXPERTS = 32
CAP = 32
POOLS = 8
POOL_ITEMS = 2048
POOL_Q = 2048
N_DP = 4


def draw_queries(key, part):
    normal_values = jax.random.normal(key, (POOLS, POOL_Q, D), jnp.float32) * 3.0
    return jnp.clip(normal_values, -18.0, 18.0).astype(jnp.bfloat16)


def with_ends(values, stream_key, smallest, top_value):
    shape = values.shape
    place = [jax.random.randint(jax.random.fold_in(stream_key, axis), (), 0, shape[axis]) for axis in range(len(shape))]
    values = values.at[tuple(place)].set(smallest)
    longest = shape.index(max(shape))
    place[longest] = (place[longest] + 1) % shape[longest]
    return values.at[tuple(place)].set(top_value)


def steps_of(stream_key, extent, cuts, low, top_value):
    def one(axis_at, blocks):
        draws = jax.random.uniform(jax.random.fold_in(jax.random.fold_in(stream_key, 6), axis_at), (blocks,), jnp.float32, low / len(cuts), top_value / len(cuts))
        return jnp.repeat(jnp.exp(draws), extent[axis_at] // blocks).reshape((-1,) + (1,) * (len(extent) - axis_at - 1))

    gain = one(*cuts[0])
    for cut in cuts[1:]:
        gain = gain * one(*cut)
    return gain


def assign_block(rng, own, number, rows, number_of, top, bound, slope):
    order = jax.random.permutation(rng, number_of)
    heavy_load, ordinary = shares(number_of, rows * top, bound, slope, True), shares(number_of, rows * top, bound, slope, False)
    places = jnp.arange(number_of)

    def named(sizes, offset_by):
        used = int((sizes > 0).sum())
        fixed = max(1, used // 4)
        shifted = fixed + (places - fixed + offset_by * (used - fixed)) % max(1, number_of - fixed)
        return jnp.zeros((number_of,), jnp.int32).at[order[jnp.where(places < fixed, places, shifted)]].set(jnp.asarray(sizes, jnp.int32))

    sizes = jnp.where(number % 4 == 0, named(heavy_load, number // 4), named(ordinary, number - number // 4 - 1))
    mixed = jax.random.permutation(jax.random.fold_in(own, 3), number_of)
    donor, receiver = mixed[0:number_of // 2 * 2:2], mixed[1:number_of // 2 * 2:2]
    slack = jnp.minimum(sizes[donor] - 1, bound - sizes[receiver]) // 2
    slack = jnp.where((donor == order[0]) | (receiver == order[0]) | (sizes[receiver] == 0), 0, jnp.maximum(slack, 0))
    shifted = jax.random.randint(jax.random.fold_in(own, 4), (number_of // 2,), 0, 1 << 20) % (slack + 1)
    sizes = sizes.at[donor].add(-shifted).at[receiver].add(shifted)
    items = jnp.searchsorted(jnp.cumsum(sizes), jnp.arange(rows * top), side="right").astype(jnp.int32)
    table = items.reshape(top, rows).T
    table = table[jax.random.permutation(jax.random.fold_in(own, 1), rows)]
    offset_by = jax.random.randint(jax.random.fold_in(own, 2), (rows, 1), 0, top)
    return jnp.take_along_axis(table, (jnp.arange(top)[None, :] + offset_by) % top, axis=1)


def shares(number_of, total, limit, slope, full):
    weights = [(1 << 20) // math.isqrt(standing ** slope) + 1 for standing in range(1, number_of + 1)]
    largest = limit if full else min(limit, max(-(-total // number_of), total * weights[0] // sum(weights)))
    least = 1 if total - largest >= number_of - 1 else 0
    given, rest = [largest] + [least] * (number_of - 1), total - largest - least * (number_of - 1)
    while rest > 0:
        free = [i for i in range(1, number_of) if given[i] < largest] or [i for i in range(1, number_of) if given[i] < limit]
        mass, budget = sum([weights[i] for i in free]), rest
        for i in free:
            extra = min(limit - given[i], max(1, budget * weights[i] // mass), rest)
            given[i] = given[i] + extra
            rest = rest - extra
    return np.array(given)


def centred(key, extent, deviation, limit, split=(), held_as=jnp.bfloat16):
    array = jax.random.normal(key, extent, jnp.float32) * deviation
    if len(split) > 0:
        array = steps_of(key, extent, split, -0.22, 0.18) * array
    return jnp.clip(array, min=-limit, max=limit).astype(held_as)


def setup_inputs(seed: int = 0) -> dict:
    arg_keys = jax.random.split(jax.random.key(seed), 9)
    item_feats = centred(arg_keys[0], (POOLS, POOL_ITEMS, D), 1.0, 6.0, ((0, 8), (1, 4)))
    expert_ids_keys = jax.random.split(jax.random.fold_in(arg_keys[1], 1), POOLS * POOL_ITEMS // ITEM_DEV)
    expert_ids_turns = jax.random.permutation(jax.random.fold_in(arg_keys[1], 3), POOLS * POOL_ITEMS // ITEM_DEV)
    expert_ids = jax.vmap(lambda own, number: assign_block(jax.random.fold_in(arg_keys[1], 2), own, number, ITEM_DEV, EXPERTS, 1, CAP, 2))(expert_ids_keys, expert_ids_turns).reshape((POOLS, POOL_ITEMS, 1))
    weight_in = centred(arg_keys[2], (EXPERTS, D, FF), D ** -0.5, 0.375, ((0, 8),))
    weight_out = centred(arg_keys[3], (EXPERTS, FF, D), FF ** -0.5, 0.1875, ((0, 8),))
    queries = draw_queries(jax.random.fold_in(arg_keys[8], 71), 0)
    query_weight = jnp.clip(jnp.exp(math.log(2.0) - 2.0794415 * jax.random.uniform(arg_keys[5], (POOLS, POOL_Q), jnp.float32) ** steps_of(arg_keys[5], (POOLS, POOL_Q), ((0, 8), (1, 4)), -0.2, 0.2)), 0.25, 2.0)
    positives = with_ends(jax.random.randint(arg_keys[6], (POOLS, POOL_Q), 0, POOL_ITEMS), jax.random.fold_in(arg_keys[6], 1), 0, POOL_ITEMS - 1).astype(jnp.int32)
    sample_counts = with_ends(jax.random.randint(arg_keys[7], (POOLS, POOL_ITEMS), 1, 4096), jax.random.fold_in(arg_keys[7], 1), 1, 4095).astype(jnp.int32)
    return dict(item_feats=item_feats, expert_ids=expert_ids, weight_in=weight_in, weight_out=weight_out, queries=queries, query_weight=query_weight, positives=positives, sample_counts=sample_counts)


norm_eps = 1e-06
block_rows = 64

def arrange(routes):
    labels = jnp.arange(EXPERTS, dtype=jnp.int32)
    onehot = (routes[:, None] == labels[None, :]).astype(jnp.int32)
    expert_loads = lax.optimization_barrier(jnp.sum(onehot, axis=0)).astype(jnp.int32)
    padded_rows = ((expert_loads + block_rows - 1) // block_rows * block_rows).astype(jnp.int32)
    range_ends = jnp.cumsum(padded_rows).astype(jnp.int32)
    starts = (range_ends - padded_rows).astype(jnp.int32)
    before = (jnp.cumsum(onehot, axis=0).astype(jnp.int32) - onehot).astype(jnp.int32)
    places = lax.optimization_barrier(jnp.sum(onehot * (before + starts[None, :]), axis=1)).astype(jnp.int32)
    blocks = (routes.shape[0] + block_rows - 1) // block_rows + EXPERTS
    firsts = jnp.arange(blocks, dtype=jnp.int32) * block_rows
    owners = lax.optimization_barrier(jnp.sum((range_ends[None, :] <= firsts[:, None]).astype(jnp.int32), axis=1))
    owners = jnp.minimum(owners, EXPERTS - 1).astype(jnp.int32)
    return (places, owners, blocks)

def rows_of(source, row_index):
    picked = lax.dynamic_slice_in_dim(source, (row_index * ITEM_DEV).astype(jnp.int32), ITEM_DEV, 1)
    return picked.reshape((POOLS * ITEM_DEV,) + source.shape[2:])

def unrows(stacked):
    shaped = stacked.reshape((N_DP, POOLS, ITEM_DEV) + stacked.shape[2:])
    return jnp.moveaxis(shaped, 0, 1).reshape((POOLS, POOL_ITEMS) + stacked.shape[2:])

def pool_half(inputs):
    pool_queries, pool_units, pool_logs, pool_weights, pool_targets = inputs
    query_block = math.gcd(POOL_Q, 1024)
    block_tally = POOL_Q // query_block
    columns = jnp.arange(POOL_ITEMS, dtype=jnp.int32)

    def query_part(parts):
        block_queries, block_weights, block_targets = parts
        scores = jnp.dot(block_queries, pool_units.T, preferred_element_type=jnp.float32) - pool_logs[None, :]
        highest = lax.optimization_barrier(jnp.max(scores, axis=1, keepdims=True))
        log_total = highest[:, 0] + jnp.log(lax.optimization_barrier(jnp.sum(jnp.exp(scores - highest), axis=1)))
        target_hit = columns[None, :] == block_targets[:, None]
        picked = lax.optimization_barrier(jnp.sum(jnp.where(target_hit, scores, 0.0), axis=1))
        mixing_factors = (block_weights[:, None] * (jnp.exp(scores - log_total[:, None]) - target_hit.astype(jnp.float32))).astype(jnp.bfloat16)
        grad_query = jnp.dot(mixing_factors, pool_units, preferred_element_type=jnp.float32)
        grad_unit = jnp.dot(mixing_factors.T, block_queries, preferred_element_type=jnp.float32)
        return (log_total - picked, grad_query, grad_unit)
    losses, grad_query, grad_unit = lax.map(query_part, (pool_queries.reshape(block_tally, query_block, D), pool_weights.reshape(block_tally, query_block), pool_targets.reshape(block_tally, query_block)))
    return (losses.reshape(POOL_Q), grad_query.reshape(POOL_Q, D), lax.optimization_barrier(jnp.sum(grad_unit, axis=0)))

def reference(item_feats, expert_ids, weight_in, weight_out, queries, query_weight, positives, sample_counts):
    features = item_feats.astype(jnp.float32)
    inv_rms = lax.rsqrt(lax.optimization_barrier(jnp.mean(features * features, axis=2, keepdims=True)) + norm_eps)
    normed = (features * inv_rms).astype(jnp.bfloat16)
    routes = expert_ids[:, :, 0]

    def forward_row(row_index):
        row_feats = rows_of(normed, row_index)
        places, owners, blocks = arrange(rows_of(routes, row_index))
        slot_rows = jnp.zeros((blocks * block_rows, D), jnp.bfloat16).at[places].set(row_feats).reshape(blocks, block_rows, D)

        def expert_block(parts):
            slot_block, owner_id = parts
            hidden = jnp.dot(slot_block, weight_in[owner_id], preferred_element_type=jnp.float32)
            active = jax.nn.gelu(hidden).astype(jnp.bfloat16)
            return jnp.dot(active, weight_out[owner_id], preferred_element_type=jnp.float32).astype(jnp.bfloat16)
        outputs = lax.map(expert_block, (slot_rows, owners))
        return outputs.reshape(blocks * block_rows, D)[places]
    branch = unrows(lax.map(forward_row, jnp.arange(N_DP, dtype=jnp.int32)))
    reduced_sum = features + branch.astype(jnp.float32)
    length = jnp.sqrt(lax.optimization_barrier(jnp.sum(reduced_sum * reduced_sum, axis=2, keepdims=True)) + norm_eps)
    unit_vecs = reduced_sum / length
    unit_low = unit_vecs.astype(jnp.bfloat16)
    log_counts = jnp.log(sample_counts.astype(jnp.float32))
    query_loss, grad_queries, grad_unit = lax.map(pool_half, (queries, unit_low, log_counts, query_weight, positives))
    along = lax.optimization_barrier(jnp.sum(unit_vecs * grad_unit, axis=2, keepdims=True))
    grad_summed = (grad_unit - unit_vecs * along) / length
    grad_low = grad_summed.astype(jnp.bfloat16)

    def backward_row(totals, row_index):
        total_in, total_out = totals
        row_feats = rows_of(normed, row_index)
        row_grads = rows_of(grad_low, row_index)
        places, owners, blocks = arrange(rows_of(routes, row_index))
        slot_feats = jnp.zeros((blocks * block_rows, D), jnp.bfloat16).at[places].set(row_feats).reshape(blocks, block_rows, D)
        slot_grads = jnp.zeros((blocks * block_rows, D), jnp.bfloat16).at[places].set(row_grads).reshape(blocks, block_rows, D)

        def expert_block(sums, parts):
            sum_in, sum_out = sums
            block_feats, block_grads, owner_id = parts
            hidden = jnp.dot(block_feats, weight_in[owner_id], preferred_element_type=jnp.float32)
            active = jax.nn.gelu(hidden).astype(jnp.bfloat16)
            grad_active = jnp.dot(block_grads, weight_out[owner_id].T, preferred_element_type=jnp.float32)
            grad_hidden = jax.vjp(jax.nn.gelu, hidden)[1](grad_active)[0].astype(jnp.bfloat16)
            grad_normed = jnp.dot(grad_hidden, weight_in[owner_id].T, preferred_element_type=jnp.float32).astype(jnp.bfloat16)
            sum_in = sum_in.at[owner_id].add(jnp.dot(block_feats.T, grad_hidden, preferred_element_type=jnp.float32))
            sum_out = sum_out.at[owner_id].add(jnp.dot(active.T, block_grads, preferred_element_type=jnp.float32))
            return ((sum_in, sum_out), grad_normed)
        start_sums = (jnp.zeros((EXPERTS, D, FF), jnp.float32), jnp.zeros((EXPERTS, FF, D), jnp.float32))
        (sum_in, sum_out), grad_normed = lax.scan(expert_block, start_sums, (slot_feats, slot_grads, owners))
        rounded_in = lax.optimization_barrier(sum_in.astype(jnp.bfloat16))
        rounded_out = lax.optimization_barrier(sum_out.astype(jnp.bfloat16))
        totals = (total_in + rounded_in.astype(jnp.float32), total_out + rounded_out.astype(jnp.float32))
        return (totals, grad_normed.reshape(blocks * block_rows, D)[places])
    start_totals = (jnp.zeros((EXPERTS, D, FF), jnp.float32), jnp.zeros((EXPERTS, FF, D), jnp.float32))
    (total_in, total_out), grad_stack = lax.scan(backward_row, start_totals, jnp.arange(N_DP, dtype=jnp.int32))
    grad_rows = unrows(grad_stack).astype(jnp.float32)
    projected = lax.optimization_barrier(jnp.mean(grad_rows * features, axis=2, keepdims=True))
    grad_items = grad_summed + inv_rms * (grad_rows - features * inv_rms * inv_rms * projected)
    return (query_loss, grad_queries, grad_items, jnp.transpose(total_in, (1, 0, 2)), jnp.transpose(total_out, (1, 0, 2)))
```

```python
import functools

import jax
import jax.numpy as jnp
from jax import lax
from jax.experimental import pallas as pl
from jax.experimental.pallas import tpu as pltpu
from jax.sharding import PartitionSpec as P

CAP = 32
norm_eps = 1e-06
BF = jnp.bfloat16
F32 = jnp.float32
GELU_C = 0.7978845608028654
GELU_A = 0.044715


def dg(a, b, ca, cb):
    return lax.dot_general(a, b, (((ca,), (cb,)), ((), ())), preferred_element_type=F32)


def iota(shape, axis):
    return lax.broadcasted_iota(jnp.int32, shape, axis)


def eye(n):
    return jnp.where(iota((n, n), 0) == iota((n, n), 1), 1.0, 0.0).astype(BF)


def to_col(row):
    n = row.shape[1]
    sub = iota((16, n), 0)
    high = lax.shift_right_logical(row, 8)
    low = lax.bitwise_and(row, 255)
    halves = jnp.where(sub == 0, high, jnp.where(sub == 1, low, 0)).astype(F32).astype(BF)
    cols = dg(eye(n), halves, 1, 1)
    return cols[:, 0:1] * 256.0 + cols[:, 1:2]


def gelu(v):
    return 0.5 * v * (1.0 + jnp.tanh(GELU_C * (v + GELU_A * v * v * v)))


def gelu_both(v):
    sq = v * v
    th = jnp.tanh(GELU_C * (v + GELU_A * v * sq))
    half = 0.5 * (1.0 + th)
    slope = half + 0.5 * v * (1.0 - th * th) * (GELU_C + (3.0 * GELU_A * GELU_C) * sq)
    return v * half, slope


def scatter_matrix(slot_row, block, rows):
    return jnp.where(iota((rows, slot_row.shape[1]), 0) + block * rows == slot_row, 1.0, 0.0).astype(BF)


def gather_rows(slot_row, blocks):
    col = to_col(slot_row).astype(jnp.int32)
    n, rows = slot_row.shape[1], blocks[0].shape[0]
    total = jnp.concatenate([b[...] for b in blocks], axis=0)
    pick = jnp.where(iota((n, rows * len(blocks)), 1) == col, 1.0, 0.0).astype(BF)
    return dg(pick, total, 1, 0)


def inv_rms_of(x):
    return lax.rsqrt(jnp.mean(x * x, axis=1, keepdims=True) + norm_eps)


def pack_kernel(local_experts, experts_all, groups, ids_ref, feats_ref, *outs):
    slot_ref, blocks = outs[0], outs[1:]
    me = lax.axis_index("expert")
    ids = ids_ref[...]
    n = ids.shape[1]
    shift = local_experts.bit_length() - 1
    hot = iota((experts_all, n), 0) == ids
    tri = jnp.where(iota((n, n), 0) < iota((n, n), 1), 1.0, 0.0).astype(BF)
    before = dg(jnp.where(hot, 1.0, 0.0).astype(BF), tri, 1, 0)
    rank = jnp.sum(jnp.where(hot, before, 0.0), axis=0, keepdims=True).astype(jnp.int32)
    owner = lax.bitwise_xor(lax.shift_right_logical(ids, shift), me)
    local = lax.bitwise_and(ids, local_experts - 1)
    slot = (owner * local_experts + local) * CAP + rank
    slot_ref[...] = slot
    x = feats_ref[...].astype(F32)
    normed = (x * inv_rms_of(x)).astype(BF)
    rows = local_experts * CAP
    for s in range(groups):
        blocks[s][...] = dg(scatter_matrix(slot, s, rows), normed, 1, 0).astype(BF)


def expert_rows(blocks, k):
    return jnp.concatenate([b[k * CAP : (k + 1) * CAP, :] for b in blocks], axis=0)


def forward_kernel(groups, win_ref, wout_ref, *refs):
    blocks, outs = refs[:groups], refs[groups:]
    for k in range(win_ref.shape[0]):
        x = expert_rows(blocks, k)
        act = gelu(dg(x, win_ref[k], 1, 0)).astype(BF)
        y = dg(act, wout_ref[k], 1, 0).astype(BF)
        for s in range(groups):
            outs[s][k * CAP : (k + 1) * CAP, :] = y[s * CAP : (s + 1) * CAP, :]


def regroup_kernel(groups, shards, *refs):
    blocks, outs = refs[:groups], refs[groups:]
    me = lax.axis_index("dp")
    for s in range(shards):
        start = pl.multiple_of(lax.bitwise_xor(me, s) * CAP, CAP)
        for g in range(groups):
            outs[s][g * CAP : (g + 1) * CAP, :] = blocks[g][pl.ds(start, CAP), :]


def log_counts_col(counts_ref, shard, rows):
    part = counts_ref[:, pl.ds(pl.multiple_of(shard * rows, 128), rows)]
    return jnp.log(to_col(part))


def unit_kernel(groups, shards, feats_ref, slot_ref, counts_ref, w_ref, pos_ref, *refs):
    blocks = refs[:groups]
    queries = refs[groups : groups + shards]
    low_ref, unit_ref, length_ref, stats_ref = refs[groups + shards :]
    rows = feats_ref.shape[0]
    branch = gather_rows(slot_ref[...], blocks)
    summed = feats_ref[...].astype(F32) + branch
    length = jnp.sqrt(jnp.sum(summed * summed, axis=1, keepdims=True) + norm_eps)
    unit = summed / length
    low = unit.astype(BF)
    low_ref[...] = low
    unit_ref[...] = unit
    length_ref[...] = jnp.broadcast_to(length, length_ref.shape)
    logs = log_counts_col(counts_ref, lax.axis_index("dp"), rows)
    for s in range(shards):
        scores = dg(low, queries[s][...], 1, 1) - logs
        high = jnp.max(scores, axis=0, keepdims=True)
        stats_ref[s : s + 1, :] = high
        stats_ref[shards + s : shards + s + 1, :] = jnp.sum(jnp.exp(scores - high), axis=0, keepdims=True)
    stats_ref[2 * shards : 2 * shards + 1, :] = w_ref[...]
    stats_ref[2 * shards + 1 : 2 * shards + 2, :] = pos_ref[...].astype(F32)


def grad_kernel(groups, shards, slot_ref, counts_ref, low_ref, unit_ref, length_ref, *refs):
    queries = refs[:shards]
    stats = refs[shards : 2 * shards]
    summed_ref, lse_ref = refs[2 * shards : 2 * shards + 2]
    outs = refs[2 * shards + 2 :]
    rows = low_ref.shape[0]
    me = lax.axis_index("dp")
    logs = log_counts_col(counts_ref, me, rows)
    low = low_ref[...]
    item = iota((rows, 1), 0) + me * rows
    total = None
    for u in range(shards):
        highs = [stats[t][(t ^ u) : (t ^ u) + 1, :] for t in range(shards)]
        sums = [stats[t][shards + (t ^ u) : shards + (t ^ u) + 1, :] for t in range(shards)]
        high = functools.reduce(jnp.maximum, highs)
        lse = high + jnp.log(sum(l * jnp.exp(m - high) for l, m in zip(sums, highs)))
        if u == 0:
            lse_ref[...] = lse
        weight = stats[u][2 * shards : 2 * shards + 1, :]
        target = stats[u][2 * shards + 1 : 2 * shards + 2, :].astype(jnp.int32)
        query = queries[u][...]
        scores = dg(low, query, 1, 1) - logs
        hit = jnp.where(item == target, 1.0, 0.0)
        coeff = (weight * (jnp.exp(scores - lse) - hit)).astype(BF)
        part = dg(coeff, query, 1, 0)
        total = part if total is None else total + part
    unit = unit_ref[...]
    along = jnp.sum(unit * total, axis=1, keepdims=True)
    summed = (total - unit * along) / length_ref[:, 0:1]
    summed_ref[...] = summed
    low_grad = summed.astype(BF)
    slot = slot_ref[...]
    for s in range(groups):
        outs[s][...] = dg(scatter_matrix(slot, s, outs[s].shape[0]), low_grad, 1, 0).astype(BF)


def query_kernel(shards, query_ref, counts_ref, lse_ref, w_ref, pos_ref, *refs):
    units = refs[:shards]
    loss_ref, grad_ref = refs[shards:]
    rows = units[0].shape[0]
    me = lax.axis_index("dp")
    query = query_ref[...]
    lse, weight, target = lse_ref[...], w_ref[...], pos_ref[...]
    picked, total = None, None
    for u in range(shards):
        shard = lax.bitwise_xor(me, u)
        unit = units[u][...]
        scores = dg(unit, query, 1, 1) - log_counts_col(counts_ref, shard, rows)
        hit = iota((rows, 1), 0) + shard * rows == target
        here = jnp.sum(jnp.where(hit, scores, 0.0), axis=0, keepdims=True)
        coeff = (weight * (jnp.exp(scores - lse) - jnp.where(hit, 1.0, 0.0))).astype(BF)
        part = dg(coeff, unit, 0, 0)
        picked = here if picked is None else picked + here
        total = part if total is None else total + part
    loss_ref[...] = lse - picked
    grad_ref[...] = total


def backward_kernel(groups, win_ref, wout_ref, *refs):
    xs, gs, outs = refs[:groups], refs[groups : 2 * groups], refs[2 * groups :]
    for k in range(win_ref.shape[0]):
        x, g = expert_rows(xs, k), expert_rows(gs, k)
        _, slope = gelu_both(dg(x, win_ref[k], 1, 0))
        hidden = (dg(g, wout_ref[k], 1, 1) * slope).astype(BF)
        y = dg(hidden, win_ref[k], 1, 1).astype(BF)
        for s in range(groups):
            outs[s][k * CAP : (k + 1) * CAP, :] = y[s * CAP : (s + 1) * CAP, :]


def early_kernel(shards, win_ref, *refs):
    xs = refs[:shards]
    act_ref, slope_ref, xt_ref = refs[shards:]
    me = lax.axis_index("dp")
    win = win_ref[me]
    width = xs[0].shape[0]
    for s in range(shards):
        x = xs[s][...]
        act, slope = gelu_both(dg(win, x, 0, 1))
        act_ref[:, s * width : (s + 1) * width] = act.astype(BF)
        slope_ref[:, s * width : (s + 1) * width] = slope.astype(BF)
        xt_ref[:, s * width : (s + 1) * width] = dg(eye(x.shape[1]), x, 1, 1).astype(BF)


def weight_out_kernel(shards, act_ref, *refs):
    gs, outs = refs[:shards], refs[shards:]
    me = lax.axis_index("dp")
    g = jnp.concatenate([r[...] for r in gs], axis=0)
    rows = act_ref.shape[0] // shards
    for s in range(shards):
        start = pl.multiple_of(lax.bitwise_xor(me, s) * rows, rows)
        outs[s][...] = dg(act_ref[pl.ds(start, rows), :], g, 1, 0).astype(BF)


def weight_in_kernel(shards, wout_ref, slope_ref, xt_ref, *refs):
    gs, outs, full = refs[:shards], refs[shards:-1], refs[-1]
    me = lax.axis_index("dp")
    g = jnp.concatenate([r[...] for r in gs], axis=0)
    hidden = (dg(wout_ref[me], g, 1, 1) * slope_ref[...].astype(F32)).astype(BF)
    full[...] = dg(xt_ref[...], hidden, 1, 1)
    rows = full.shape[0] // shards
    for s in range(shards):
        start = pl.multiple_of(lax.bitwise_xor(me, s) * rows, rows)
        outs[s][...] = full[pl.ds(start, rows), :].astype(BF)


def final_kernel(groups, feats_ref, slot_ref, summed_ref, *refs):
    blocks, out_ref = refs[:groups], refs[groups]
    x = feats_ref[...].astype(F32)
    r = inv_rms_of(x)
    rows = gather_rows(slot_ref[...], blocks)
    projected = jnp.mean(rows * x, axis=1, keepdims=True)
    out_ref[...] = summed_ref[...] + r * (rows - x * (r * r) * projected)


def call(body, outs, args, flops=0, touched=0, trans=0, scratch=()):
    shapes = [jax.ShapeDtypeStruct(s, d) for s, d in outs]
    return pl.pallas_call(
        body,
        out_shape=shapes,
        in_specs=[pl.BlockSpec(memory_space=pltpu.VMEM)] * len(args),
        out_specs=[pl.BlockSpec(memory_space=pltpu.VMEM)] * len(outs),
        scratch_shapes=list(scratch),
        cost_estimate=pl.CostEstimate(flops=flops, bytes_accessed=touched, transcendentals=trans),
        name=body.func.__name__,
    )(*args)


def shift_by(values, axis, s):
    n = lax.axis_size(axis)
    return lax.ppermute(values, axis, [(i, i ^ s) for i in range(n)])


def exchange(blocks, axis):
    return [blocks[0]] + [shift_by(b, axis, s) for s, b in enumerate(blocks) if s > 0]


def spread(block, axis):
    return [block] + [shift_by(block, axis, s) for s in range(1, lax.axis_size(axis))]


def per_device(
    item_feats, expert_ids, weight_in, weight_out, queries, query_weight, positives, sample_counts
):
    groups, shards = lax.axis_size("expert"), lax.axis_size("dp")
    local_experts, width, units = weight_in.shape
    rows, q_rows = item_feats.shape[1], queries.shape[1]
    experts_all = local_experts * groups
    feats = item_feats[0]
    ids = expert_ids.reshape(1, rows)
    slots = local_experts * CAP
    query = queries[0]
    block = ((slots, width), BF)
    matmul = 2 * rows * q_rows * shards * width
    expert_flops = 2 * groups * slots * width * units

    slot, *packed = call(
        functools.partial(pack_kernel, local_experts, experts_all, groups),
        [((1, rows), jnp.int32)] + [block] * groups,
        (ids, feats),
        flops=2 * groups * slots * rows * width,
        touched=1 << 20,
    )
    received = exchange(packed, "expert")
    all_queries = spread(query, "dp")
    output = call(
        functools.partial(forward_kernel, groups),
        [block] * groups,
        (weight_in, weight_out, *received),
        flops=2 * expert_flops,
        touched=6 << 20,
        trans=groups * slots * units,
    )
    returned = exchange(output, "expert")
    low, unit, length, stats = call(
        functools.partial(unit_kernel, groups, shards),
        [
            ((rows, width), BF),
            ((rows, width), F32),
            ((rows, 128), F32),
            ((2 * shards + 2, q_rows), F32),
        ],
        (feats, slot, sample_counts, query_weight, positives, *returned, *all_queries),
        flops=2 * matmul,
        touched=4 << 20,
        trans=rows * q_rows * shards,
    )
    all_stats = spread(stats, "dp")
    summed, lse, *packed_grads = call(
        functools.partial(grad_kernel, groups, shards),
        [((rows, width), F32), ((1, q_rows), F32)] + [block] * groups,
        (slot, sample_counts, low, unit, length, *all_queries, *all_stats),
        flops=3 * matmul,
        touched=4 << 20,
        trans=rows * q_rows * shards,
    )
    received_grads = exchange(packed_grads, "expert")
    low, lse = lax.optimization_barrier((low, lse))
    all_units = spread(low, "dp")
    query_loss, grad_queries = call(
        functools.partial(query_kernel, shards),
        [((1, q_rows), F32), ((q_rows, width), F32)],
        (query, sample_counts, lse, query_weight, positives, *all_units),
        flops=2 * matmul,
        touched=3 << 20,
        trans=rows * q_rows * shards,
    )
    grad_out = call(
        functools.partial(backward_kernel, groups),
        [block] * groups,
        (weight_in, weight_out, *received, *received_grads),
        flops=3 * expert_flops,
        touched=6 << 20,
        trans=groups * slots * units,
    )
    grad_back = exchange(grad_out, "expert")
    (grad_items,) = call(
        functools.partial(final_kernel, groups),
        [((rows, width), F32)],
        (feats, slot, summed, *grad_back),
        flops=2 * groups * slots * rows * width,
        touched=2 << 20,
    )
    if shards == local_experts:
        tokens = ((groups * CAP, width), BF)
        regroup = functools.partial(regroup_kernel, groups, shards)
        own_x = exchange(call(regroup, [tokens] * shards, received, touched=1 << 20), "dp")
        total_rows = shards * groups * CAP
        act, slope, xt = call(
            functools.partial(early_kernel, shards),
            [((units, total_rows), BF), ((units, total_rows), BF), ((width, total_rows), BF)],
            (weight_in, *own_x),
            flops=expert_flops,
            touched=6 << 20,
            trans=total_rows * units,
        )
        own_g = exchange(call(regroup, [tokens] * shards, received_grads, touched=1 << 20), "dp")
        out_parts = exchange(
            call(
                functools.partial(weight_out_kernel, shards),
                [((units // shards, width), BF)] * shards,
                (act, *own_g),
                flops=expert_flops,
                touched=3 << 20,
            ),
            "dp",
        )
        in_parts = exchange(
            call(
                functools.partial(weight_in_kernel, shards),
                [((width // shards, units), BF)] * shards,
                (weight_out, slope, xt, *own_g),
                flops=2 * expert_flops,
                touched=4 << 20,
                scratch=[pltpu.VMEM((width, units), F32)],
            ),
            "dp",
        )
        me = lax.axis_index("dp")

        def assemble(parts):
            ordered = []
            for k in range(local_experts):
                source = lax.bitwise_xor(me, k)
                value = parts[0]
                for s in range(1, shards):
                    value = jnp.where(source == s, parts[s], value)
                ordered.append(value)
            return jnp.stack(ordered, axis=1).astype(F32)

        grad_weight_in, grad_weight_out = assemble(in_parts), assemble(out_parts)
    else:
        x = jnp.stack(received).reshape(groups, local_experts, CAP, width)
        g = jnp.stack(received_grads).reshape(groups, local_experts, CAP, width)
        hidden = jnp.einsum("skcd,kdf->skcf", x, weight_in, preferred_element_type=F32)
        active, slope = gelu_both(hidden)
        grad_active = jnp.einsum("skcd,kfd->skcf", g, weight_out, preferred_element_type=F32)
        grad_hidden = (grad_active * slope).astype(BF)

        def reduce(a, b):
            part = jnp.einsum("skcr,skcf->rkf", a, b, preferred_element_type=F32).astype(BF)
            return lax.psum_scatter(part, "dp", scatter_dimension=0, tiled=True).astype(F32)

        grad_weight_in, grad_weight_out = reduce(x, grad_hidden), reduce(active.astype(BF), g)
    return (query_loss, grad_queries[None], grad_items[None], grad_weight_in, grad_weight_out)


def solution(mesh):
    placed = (
        P("expert", "dp", None),
        P("expert", "dp", None),
        P("expert", None, None),
        P("expert", None, None),
        P("expert", "dp", None),
        P("expert", "dp"),
        P("expert", "dp"),
        P("expert", None),
    )
    return jax.shard_map(
        per_device,
        mesh=mesh,
        in_specs=placed,
        out_specs=(
            P("expert", "dp"),
            P("expert", "dp", None),
            P("expert", "dp", None),
            P("dp", "expert", None),
            P("dp", "expert", None),
        ),
        check_vma=False,
    )
```

```python
import functools

import jax
import jax.numpy as jnp
from jax import lax
from jax.experimental import pallas as pl
from jax.experimental.pallas import tpu as pltpu
from jax.sharding import PartitionSpec as P

CAP = 32
norm_eps = 1e-06
BF = jnp.bfloat16
F32 = jnp.float32
GELU_C = 0.7978845608028654
GELU_A = 0.044715


def dg(a, b, ca, cb):
    return lax.dot_general(a, b, (((ca,), (cb,)), ((), ())), preferred_element_type=F32)


def iota(shape, axis):
    return lax.broadcasted_iota(jnp.int32, shape, axis)


def eye(n):
    return jnp.where(iota((n, n), 0) == iota((n, n), 1), 1.0, 0.0).astype(BF)


def to_col(row):
    n = row.shape[1]
    sub = iota((16, n), 0)
    high = lax.shift_right_logical(row, 8)
    low = lax.bitwise_and(row, 255)
    halves = jnp.where(sub == 0, high, jnp.where(sub == 1, low, 0)).astype(F32).astype(BF)
    cols = dg(eye(n), halves, 1, 1)
    return cols[:, 0:1] * 256.0 + cols[:, 1:2]


def gelu(v):
    return 0.5 * v * (1.0 + jnp.tanh(GELU_C * (v + GELU_A * v * v * v)))


def gelu_both(v):
    sq = v * v
    th = jnp.tanh(GELU_C * (v + GELU_A * v * sq))
    half = 0.5 * (1.0 + th)
    slope = half + 0.5 * v * (1.0 - th * th) * (GELU_C + (3.0 * GELU_A * GELU_C) * sq)
    return v * half, slope


def scatter_matrix(slot_row, block, rows):
    return jnp.where(iota((rows, slot_row.shape[1]), 0) + block * rows == slot_row, 1.0, 0.0).astype(BF)


def gather_rows(slot_row, blocks):
    col = to_col(slot_row).astype(jnp.int32)
    n, rows = slot_row.shape[1], blocks[0].shape[0]
    total = jnp.concatenate([b[...] for b in blocks], axis=0)
    pick = jnp.where(iota((n, rows * len(blocks)), 1) == col, 1.0, 0.0).astype(BF)
    return dg(pick, total, 1, 0)


def inv_rms_of(x):
    return lax.rsqrt(jnp.mean(x * x, axis=1, keepdims=True) + norm_eps)


def pack_kernel(local_experts, experts_all, groups, ids_hbm, feats_hbm, *refs):
    slot_ref, blocks = refs[0], refs[1 : groups + 1]
    ids_ref, feats_ref, ids_sem, feats_sem = refs[groups + 1 :]
    ids_copy = pltpu.make_async_copy(ids_hbm, ids_ref, ids_sem)
    feats_copy = pltpu.make_async_copy(feats_hbm, feats_ref, feats_sem)
    ids_copy.start()
    feats_copy.start()
    me = lax.axis_index("expert")
    ids_copy.wait()
    ids = ids_ref[...]
    n = ids.shape[1]
    shift = local_experts.bit_length() - 1
    hot = iota((experts_all, n), 0) == ids
    tri = jnp.where(iota((n, n), 0) < iota((n, n), 1), 1.0, 0.0).astype(BF)
    before = dg(jnp.where(hot, 1.0, 0.0).astype(BF), tri, 1, 0)
    rank = jnp.sum(jnp.where(hot, before, 0.0), axis=0, keepdims=True).astype(jnp.int32)
    owner = lax.bitwise_xor(lax.shift_right_logical(ids, shift), me)
    local = lax.bitwise_and(ids, local_experts - 1)
    slot = (owner * local_experts + local) * CAP + rank
    slot_ref[...] = slot
    feats_copy.wait()
    x = feats_ref[...].astype(F32)
    normed = (x * inv_rms_of(x)).astype(BF)
    rows = local_experts * CAP
    for s in range(groups):
        blocks[s][...] = dg(scatter_matrix(slot, s, rows), normed, 1, 0).astype(BF)


def load_kernel(win_hbm, wout_hbm, win_ref, wout_ref, in_sem, out_sem):
    copies = (
        pltpu.make_async_copy(win_hbm, win_ref, in_sem),
        pltpu.make_async_copy(wout_hbm, wout_ref, out_sem),
    )
    for copy in copies:
        copy.start()
    for copy in copies:
        copy.wait()


def expert_rows(blocks, k):
    return jnp.concatenate([b[k * CAP : (k + 1) * CAP, :] for b in blocks], axis=0)


def forward_kernel(groups, win_ref, wout_ref, *refs):
    blocks, outs = refs[:groups], refs[groups:]
    for k in range(win_ref.shape[0]):
        x = expert_rows(blocks, k)
        act = gelu(dg(x, win_ref[k], 1, 0)).astype(BF)
        y = dg(act, wout_ref[k], 1, 0).astype(BF)
        for s in range(groups):
            outs[s][k * CAP : (k + 1) * CAP, :] = y[s * CAP : (s + 1) * CAP, :]


def slope_kernel(groups, win_ref, *refs):
    blocks, slope_ref = refs[:groups], refs[groups]
    for k in range(win_ref.shape[0]):
        _, slope = gelu_both(dg(expert_rows(blocks, k), win_ref[k], 1, 0))
        slope_ref[k] = slope


def regroup_kernel(groups, shards, *refs):
    blocks, outs = refs[:groups], refs[groups:]
    me = lax.axis_index("dp")
    for s in range(shards):
        start = pl.multiple_of(lax.bitwise_xor(me, s) * CAP, CAP)
        for g in range(groups):
            outs[s][g * CAP : (g + 1) * CAP, :] = blocks[g][pl.ds(start, CAP), :]


def log_counts_col(counts_ref, shard, rows):
    part = counts_ref[:, pl.ds(pl.multiple_of(shard * rows, 128), rows)]
    return jnp.log(to_col(part))


def unit_kernel(groups, shards, feats_ref, slot_ref, counts_ref, w_ref, pos_ref, *refs):
    blocks = refs[:groups]
    queries = refs[groups : groups + shards]
    low_ref, unit_ref, length_ref, stats_ref, terms_ref = refs[groups + shards :]
    rows = feats_ref.shape[0]
    branch = gather_rows(slot_ref[...], blocks)
    summed = feats_ref[...].astype(F32) + branch
    length = jnp.sqrt(jnp.sum(summed * summed, axis=1, keepdims=True) + norm_eps)
    unit = summed / length
    low = unit.astype(BF)
    low_ref[...] = low
    unit_ref[...] = unit
    length_ref[...] = jnp.broadcast_to(length, length_ref.shape)
    logs = log_counts_col(counts_ref, lax.axis_index("dp"), rows)
    for s in range(shards):
        scores = dg(low, queries[s][...], 1, 1) - logs
        high = jnp.max(scores, axis=0, keepdims=True)
        stats_ref[s : s + 1, :] = high
        terms = jnp.exp(scores - high)
        terms_ref[s] = terms
        stats_ref[shards + s : shards + s + 1, :] = jnp.sum(terms, axis=0, keepdims=True)
    stats_ref[2 * shards : 2 * shards + 1, :] = w_ref[...]
    stats_ref[2 * shards + 1 : 2 * shards + 2, :] = pos_ref[...].astype(F32)


def grad_kernel(groups, shards, slot_ref, unit_ref, length_ref, terms_ref, *refs):
    queries = refs[:shards]
    stats = refs[shards : 2 * shards]
    summed_ref, lse_ref = refs[2 * shards : 2 * shards + 2]
    outs = refs[2 * shards + 2 :]
    rows = unit_ref.shape[0]
    item = iota((rows, 1), 0) + lax.axis_index("dp") * rows
    total = None
    for u in range(shards):
        highs = [stats[t][(t ^ u) : (t ^ u) + 1, :] for t in range(shards)]
        sums = [stats[t][shards + (t ^ u) : shards + (t ^ u) + 1, :] for t in range(shards)]
        high = functools.reduce(jnp.maximum, highs)
        lse = high + jnp.log(sum(l * jnp.exp(m - high) for l, m in zip(sums, highs)))
        if u == 0:
            lse_ref[...] = lse
        weight = stats[u][2 * shards : 2 * shards + 1, :]
        target = stats[u][2 * shards + 1 : 2 * shards + 2, :].astype(jnp.int32)
        scale = weight * jnp.exp(highs[0] - lse)
        coeff = (terms_ref[u] * scale - jnp.where(item == target, weight, 0.0)).astype(BF)
        part = dg(coeff, queries[u][...], 1, 0)
        total = part if total is None else total + part
    unit = unit_ref[...]
    along = jnp.sum(unit * total, axis=1, keepdims=True)
    summed = (total - unit * along) / length_ref[:, 0:1]
    summed_ref[...] = summed
    low_grad = summed.astype(BF)
    slot = slot_ref[...]
    for s in range(groups):
        outs[s][...] = dg(scatter_matrix(slot, s, outs[s].shape[0]), low_grad, 1, 0).astype(BF)


def turned(row):
    return jnp.transpose(jnp.broadcast_to(row, (128, row.shape[1])))


def query_kernel(shards, query_ref, counts_ref, lse_ref, w_ref, pos_ref, *refs):
    units = refs[:shards]
    loss_ref, grad_ref = refs[shards:]
    rows = units[0].shape[0]
    me = lax.axis_index("dp")
    query = query_ref[...]
    lse, weight = turned(lse_ref[...])[:, 0:1], turned(w_ref[...])[:, 0:1]
    target = turned(pos_ref[...].astype(F32))[:, 0:1].astype(jnp.int32)
    picked, total = None, None
    for u in range(shards):
        shard = lax.bitwise_xor(me, u)
        unit = units[u][...]
        counts = counts_ref[:, pl.ds(pl.multiple_of(shard * rows, 128), rows)]
        scores = dg(query, unit, 1, 1) - jnp.log(counts.astype(F32))
        hit = iota((1, rows), 1) + shard * rows == target
        here = jnp.sum(jnp.where(hit, scores, 0.0), axis=1, keepdims=True)
        coeff = (weight * (jnp.exp(scores - lse) - jnp.where(hit, 1.0, 0.0))).astype(BF)
        part = dg(coeff, unit, 1, 0)
        picked = here if picked is None else picked + here
        total = part if total is None else total + part
    loss = jnp.broadcast_to(lse - picked, (query.shape[0], 128))
    loss_ref[...] = jnp.transpose(loss)[0:1, :]
    grad_ref[...] = total


def backward_kernel(groups, win_ref, wout_ref, slope_ref, *refs):
    gs, outs = refs[:groups], refs[groups:]
    for k in range(win_ref.shape[0]):
        hidden = (dg(expert_rows(gs, k), wout_ref[k], 1, 1) * slope_ref[k]).astype(BF)
        y = dg(hidden, win_ref[k], 1, 1).astype(BF)
        for s in range(groups):
            outs[s][k * CAP : (k + 1) * CAP, :] = y[s * CAP : (s + 1) * CAP, :]


def early_kernel(shards, win_ref, *refs):
    xs = refs[:shards]
    act_ref, slope_ref, xt_ref = refs[shards:]
    me = lax.axis_index("dp")
    win = win_ref[me]
    width = xs[0].shape[0]
    for s in range(shards):
        x = xs[s][...]
        act, slope = gelu_both(dg(win, x, 0, 1))
        act_ref[:, s * width : (s + 1) * width] = act.astype(BF)
        slope_ref[:, s * width : (s + 1) * width] = slope.astype(BF)
        xt_ref[:, s * width : (s + 1) * width] = dg(eye(x.shape[1]), x, 1, 1).astype(BF)


def weight_kernel(shards, wout_ref, act_ref, slope_ref, xt_ref, *refs):
    gs, outs, full = refs[:shards], refs[shards:-1], refs[-1]
    me = lax.axis_index("dp")
    g = jnp.concatenate([r[...] for r in gs], axis=0)
    width = g.shape[1]
    hidden = (dg(wout_ref[me], g, 1, 1) * slope_ref[...].astype(F32)).astype(BF)
    full[...] = dg(xt_ref[...], hidden, 1, 1)
    out_rows, in_rows = act_ref.shape[0] // shards, full.shape[0] // shards
    for s in range(shards):
        peer = lax.bitwise_xor(me, s)
        start = pl.multiple_of(peer * out_rows, out_rows)
        outs[s][:out_rows, :] = dg(act_ref[pl.ds(start, out_rows), :], g, 1, 0).astype(BF)
        start = pl.multiple_of(peer * in_rows, in_rows)
        for c in range(full.shape[1] // width):
            piece = full[pl.ds(start, in_rows), c * width : (c + 1) * width]
            first = out_rows + c * in_rows
            outs[s][first : first + in_rows, :] = piece.astype(BF)


def assemble_kernel(shards, *refs):
    parts, (in_ref, out_ref) = refs[:shards], refs[shards:]
    me = lax.axis_index("dp")
    in_rows, experts, units = in_ref.shape
    out_rows, _, width = out_ref.shape
    size = in_rows * experts
    row, col = iota((size, size), 0), iota((size, size), 1)
    bits = experts.bit_length() - 1
    wanted = lax.bitwise_xor(lax.bitwise_and(row, experts - 1), me) * in_rows
    spread_rows = jnp.where(wanted + lax.shift_right_logical(row, bits) == col, 1.0, 0.0).astype(BF)
    for c in range(units // width):
        first = out_rows + c * in_rows
        stacked = jnp.concatenate([r[first : first + in_rows, :] for r in parts], axis=0)
        block = dg(spread_rows, stacked, 1, 0)
        in_ref[:, :, c * width : (c + 1) * width] = block.reshape(in_rows, experts, width)
    for c in range(out_rows // in_rows):
        first = c * in_rows
        stacked = jnp.concatenate([r[first : first + in_rows, :] for r in parts], axis=0)
        block = dg(spread_rows, stacked, 1, 0)
        out_ref[first : first + in_rows] = block.reshape(in_rows, experts, width)


def final_kernel(groups, feats_ref, slot_ref, summed_ref, *refs):
    blocks, out_ref = refs[:groups], refs[groups]
    x = feats_ref[...].astype(F32)
    r = inv_rms_of(x)
    rows = gather_rows(slot_ref[...], blocks)
    projected = jnp.mean(rows * x, axis=1, keepdims=True)
    out_ref[...] = summed_ref[...] + r * (rows - x * (r * r) * projected)


def call(body, outs, args, flops=0, touched=0, trans=0, scratch=(), space=pltpu.VMEM, limit=24):
    shapes = [jax.ShapeDtypeStruct(s, d) for s, d in outs]
    return pl.pallas_call(
        body,
        out_shape=shapes,
        in_specs=[pl.BlockSpec(memory_space=space)] * len(args),
        out_specs=[pl.BlockSpec(memory_space=pltpu.VMEM)] * len(outs),
        scratch_shapes=list(scratch),
        cost_estimate=pl.CostEstimate(flops=flops, bytes_accessed=touched, transcendentals=trans),
        compiler_params=pltpu.CompilerParams(vmem_limit_bytes=limit << 20),
    )(*args)


def shift_by(values, axis, s):
    n = lax.axis_size(axis)
    return lax.ppermute(values, axis, [(i, i ^ s) for i in range(n)])


def exchange(blocks, axis):
    return [blocks[0]] + [shift_by(b, axis, s) for s, b in enumerate(blocks) if s > 0]


def spread(block, axis):
    return exchange([block] * lax.axis_size(axis), axis)


def per_device(
    item_feats, expert_ids, weight_in, weight_out, queries, query_weight, positives, sample_counts
):
    groups, shards = lax.axis_size("expert"), lax.axis_size("dp")
    local_experts, width, units = weight_in.shape
    rows, q_rows = item_feats.shape[1], queries.shape[1]
    experts_all = local_experts * groups
    feats = item_feats[0]
    ids = expert_ids.reshape(1, rows)
    slots = local_experts * CAP
    query = queries[0]
    block = ((slots, width), BF)
    matmul = 2 * rows * q_rows * shards * width
    expert_flops = 2 * groups * slots * width * units

    slot, *packed = call(
        functools.partial(pack_kernel, local_experts, experts_all, groups),
        [((1, rows), jnp.int32)] + [block] * groups,
        (ids, feats),
        flops=2 * groups * slots * rows * width,
        touched=1 << 20,
        scratch=[
            pltpu.VMEM((1, rows), jnp.int32),
            pltpu.VMEM((rows, width), BF),
            pltpu.SemaphoreType.DMA(()),
            pltpu.SemaphoreType.DMA(()),
        ],
        space=pltpu.HBM,
        limit=60,
    )
    received = exchange(packed, "expert")
    all_queries = spread(query, "dp")
    weight_in, weight_out = call(
        load_kernel,
        [(weight_in.shape, BF), (weight_out.shape, BF)],
        (weight_in, weight_out),
        touched=16 << 20,
        scratch=[pltpu.SemaphoreType.DMA(()), pltpu.SemaphoreType.DMA(())],
        space=pltpu.HBM,
    )
    output = call(
        functools.partial(forward_kernel, groups),
        [block] * groups,
        (weight_in, weight_out, *received),
        flops=2 * expert_flops,
        touched=6 << 20,
        trans=groups * slots * units,
    )
    returned = exchange(output, "expert")
    (slope,) = call(
        functools.partial(slope_kernel, groups),
        [((local_experts, groups * CAP, units), F32)],
        (weight_in, *received),
        flops=expert_flops,
        touched=6 << 20,
        trans=groups * slots * units,
    )
    low, unit, length, stats, terms = call(
        functools.partial(unit_kernel, groups, shards),
        [
            ((rows, width), BF),
            ((rows, width), F32),
            ((rows, 128), F32),
            ((2 * shards + 2, q_rows), F32),
            ((shards, rows, q_rows), F32),
        ],
        (feats, slot, sample_counts, query_weight, positives, *returned, *all_queries),
        flops=2 * matmul,
        touched=4 << 20,
        trans=rows * q_rows * shards,
    )
    all_stats = spread(stats, "dp")
    summed, lse, *packed_grads = call(
        functools.partial(grad_kernel, groups, shards),
        [((rows, width), F32), ((1, q_rows), F32)] + [block] * groups,
        (slot, unit, length, terms, *all_queries, *all_stats),
        flops=3 * matmul,
        touched=4 << 20,
        trans=rows * q_rows * shards,
    )
    received_grads = exchange(packed_grads, "expert")
    all_units = spread(low, "dp")
    query_loss, grad_queries = call(
        functools.partial(query_kernel, shards),
        [((1, q_rows), F32), ((q_rows, width), F32)],
        (query, sample_counts, lse, query_weight, positives, *all_units),
        flops=2 * matmul,
        touched=3 << 20,
        trans=rows * q_rows * shards,
    )
    grad_out = call(
        functools.partial(backward_kernel, groups),
        [block] * groups,
        (weight_in, weight_out, slope, *received_grads),
        flops=2 * expert_flops,
        touched=6 << 20,
        trans=groups * slots * units,
    )
    grad_back = exchange(grad_out, "expert")
    (grad_items,) = call(
        functools.partial(final_kernel, groups),
        [((rows, width), F32)],
        (feats, slot, summed, *grad_back),
        flops=2 * groups * slots * rows * width,
        touched=2 << 20,
    )
    if shards == local_experts:
        tokens = ((groups * CAP, width), BF)
        regroup = functools.partial(regroup_kernel, groups, shards)
        own_x = exchange(call(regroup, [tokens] * shards, received, touched=1 << 20), "dp")
        total_rows = shards * groups * CAP
        act, act_slope, xt = call(
            functools.partial(early_kernel, shards),
            [((units, total_rows), BF), ((units, total_rows), BF), ((width, total_rows), BF)],
            (weight_in, *own_x),
            flops=expert_flops,
            touched=6 << 20,
            trans=total_rows * units,
        )
        own_g = exchange(call(regroup, [tokens] * shards, received_grads, touched=1 << 20), "dp")
        parts = exchange(
            call(
                functools.partial(weight_kernel, shards),
                [((units // shards + units // shards, width), BF)] * shards,
                (weight_out, act, act_slope, xt, *own_g),
                flops=3 * expert_flops,
                touched=6 << 20,
                scratch=[pltpu.VMEM((width, units), F32)],
            ),
            "dp",
        )
        grad_weight_in, grad_weight_out = call(
            functools.partial(assemble_kernel, shards),
            [
                ((width // shards, local_experts, units), F32),
                ((units // shards, local_experts, width), F32),
            ],
            parts,
            flops=expert_flops,
            touched=6 << 20,
        )
    else:
        x = jnp.stack(received).reshape(groups, local_experts, CAP, width)
        g = jnp.stack(received_grads).reshape(groups, local_experts, CAP, width)
        hidden = jnp.einsum("skcd,kdf->skcf", x, weight_in, preferred_element_type=F32)
        active, slope = gelu_both(hidden)
        grad_active = jnp.einsum("skcd,kfd->skcf", g, weight_out, preferred_element_type=F32)
        grad_hidden = (grad_active * slope).astype(BF)

        def reduce(a, b):
            part = jnp.einsum("skcr,skcf->rkf", a, b, preferred_element_type=F32).astype(BF)
            return lax.psum_scatter(part, "dp", scatter_dimension=0, tiled=True).astype(F32)

        grad_weight_in, grad_weight_out = reduce(x, grad_hidden), reduce(active.astype(BF), g)
    return (query_loss, grad_queries[None], grad_items[None], grad_weight_in, grad_weight_out)


def solution(mesh):
    placed = (
        P("expert", "dp", None),
        P("expert", "dp", None),
        P("expert", None, None),
        P("expert", None, None),
        P("expert", "dp", None),
        P("expert", "dp"),
        P("expert", "dp"),
        P("expert", None),
    )

    return jax.shard_map(
        per_device,
        mesh=mesh,
        in_specs=placed,
        out_specs=(
            P("expert", "dp"),
            P("expert", "dp", None),
            P("expert", "dp", None),
            P("dp", "expert", None),
            P("dp", "expert", None),
        ),
        check_vma=False,
    )
```

```python
import functools

import jax
import jax.numpy as jnp
from jax import lax
from jax.experimental import pallas as pl
from jax.experimental.pallas import tpu as pltpu
from jax.sharding import PartitionSpec as P

CAP = 32
norm_eps = 1e-06
BF = jnp.bfloat16
F32 = jnp.float32
GELU_C = 0.7978845608028654
GELU_A = 0.044715


def dg(a, b, ca, cb):
    return lax.dot_general(a, b, (((ca,), (cb,)), ((), ())), preferred_element_type=F32)


def iota(shape, axis):
    return lax.broadcasted_iota(jnp.int32, shape, axis)


def eye(n):
    return jnp.where(iota((n, n), 0) == iota((n, n), 1), 1.0, 0.0).astype(BF)


def to_col(row):
    n = row.shape[1]
    sub = iota((16, n), 0)
    high = lax.shift_right_logical(row, 8)
    low = lax.bitwise_and(row, 255)
    halves = jnp.where(sub == 0, high, jnp.where(sub == 1, low, 0)).astype(F32).astype(BF)
    cols = dg(eye(n), halves, 1, 1)
    return cols[:, 0:1] * 256.0 + cols[:, 1:2]


def gelu(v):
    return 0.5 * v * (1.0 + jnp.tanh(GELU_C * (v + GELU_A * v * v * v)))


def gelu_both(v):
    sq = v * v
    th = jnp.tanh(GELU_C * (v + GELU_A * v * sq))
    half = 0.5 * (1.0 + th)
    slope = half + 0.5 * v * (1.0 - th * th) * (GELU_C + (3.0 * GELU_A * GELU_C) * sq)
    return v * half, slope


def scatter_matrix(slot_row, block, rows):
    return jnp.where(iota((rows, slot_row.shape[1]), 0) + block * rows == slot_row, 1.0, 0.0).astype(BF)


def gather_rows(pick_ref, blocks):
    return dg(pick_ref[...], jnp.concatenate([b[...] for b in blocks], axis=0), 1, 0)


def inv_rms_of(x):
    return lax.rsqrt(jnp.mean(x * x, axis=1, keepdims=True) + norm_eps)


def pack_kernel(local_experts, experts_all, groups, ids_hbm, feats_hbm, *refs):
    slot_ref, blocks = refs[0], refs[1 : groups + 1]
    ids_ref, feats_ref, ids_sem, feats_sem = refs[groups + 1 :]
    ids_copy = pltpu.make_async_copy(ids_hbm, ids_ref, ids_sem)
    feats_copy = pltpu.make_async_copy(feats_hbm, feats_ref, feats_sem)
    ids_copy.start()
    feats_copy.start()
    me = lax.axis_index("expert")
    ids_copy.wait()
    ids = ids_ref[...]
    n = ids.shape[1]
    shift = local_experts.bit_length() - 1
    hot = iota((experts_all, n), 0) == ids
    tri = jnp.where(iota((n, n), 0) < iota((n, n), 1), 1.0, 0.0).astype(BF)
    before = dg(jnp.where(hot, 1.0, 0.0).astype(BF), tri, 1, 0)
    rank = jnp.sum(jnp.where(hot, before, 0.0), axis=0, keepdims=True).astype(jnp.int32)
    owner = lax.bitwise_xor(lax.shift_right_logical(ids, shift), me)
    local = lax.bitwise_and(ids, local_experts - 1)
    slot = (owner * local_experts + local) * CAP + rank
    slot_ref[...] = slot
    feats_copy.wait()
    x = feats_ref[...].astype(F32)
    normed = (x * inv_rms_of(x)).astype(BF)
    rows = local_experts * CAP
    for s in range(groups):
        blocks[s][...] = dg(scatter_matrix(slot, s, rows), normed, 1, 0).astype(BF)


def load_kernel(
    win_hbm, wout_hbm, slot_ref, counts_ref, win_ref, wout_ref, pick_ref, put_ref, logs_ref, in_sem, out_sem
):
    copies = (
        pltpu.make_async_copy(win_hbm, win_ref, in_sem),
        pltpu.make_async_copy(wout_hbm, wout_ref, out_sem),
    )
    for copy in copies:
        copy.start()
    slot = slot_ref[...]
    col = to_col(slot).astype(jnp.int32)
    pick_ref[...] = jnp.where(iota(pick_ref.shape, 1) == col, 1.0, 0.0).astype(BF)
    put_ref[...] = scatter_matrix(slot, 0, put_ref.shape[0])
    logs = log_counts_col(counts_ref, lax.axis_index("dp"), slot.shape[1])
    logs_ref[...] = jnp.broadcast_to(logs, logs_ref.shape)
    for copy in copies:
        copy.wait()


def expert_rows(blocks, k):
    return jnp.concatenate([b[k * CAP : (k + 1) * CAP, :] for b in blocks], axis=0)


def forward_kernel(groups, win_ref, wout_ref, *refs):
    blocks, outs = refs[:groups], refs[groups:]
    for k in range(win_ref.shape[0]):
        x = expert_rows(blocks, k)
        act = gelu(dg(x, win_ref[k], 1, 0)).astype(BF)
        y = dg(act, wout_ref[k], 1, 0).astype(BF)
        for s in range(groups):
            outs[s][k * CAP : (k + 1) * CAP, :] = y[s * CAP : (s + 1) * CAP, :]


def slope_kernel(groups, win_ref, *refs):
    blocks, slope_ref = refs[:groups], refs[groups]
    for k in range(win_ref.shape[0]):
        _, slope = gelu_both(dg(expert_rows(blocks, k), win_ref[k], 1, 0))
        slope_ref[k] = slope


def regroup_kernel(groups, shards, *refs):
    blocks, outs = refs[:groups], refs[groups:]
    me = lax.axis_index("dp")
    for s in range(shards):
        start = pl.multiple_of(lax.bitwise_xor(me, s) * CAP, CAP)
        for g in range(groups):
            outs[s][g * CAP : (g + 1) * CAP, :] = blocks[g][pl.ds(start, CAP), :]


def log_counts_col(counts_ref, shard, rows):
    part = counts_ref[:, pl.ds(pl.multiple_of(shard * rows, 128), rows)]
    return jnp.log(to_col(part))


def unit_kernel(groups, shards, feats_ref, pick_ref, logs_ref, w_ref, pos_ref, *refs):
    blocks = refs[:groups]
    queries = refs[groups : groups + shards]
    low_ref, unit_ref, length_ref, stats_ref, terms_ref = refs[groups + shards :]
    branch = gather_rows(pick_ref, blocks)
    summed = feats_ref[...].astype(F32) + branch
    length = jnp.sqrt(jnp.sum(summed * summed, axis=1, keepdims=True) + norm_eps)
    unit = summed / length
    low = unit.astype(BF)
    low_ref[...] = low
    unit_ref[...] = unit
    length_ref[...] = jnp.broadcast_to(length, length_ref.shape)
    logs = logs_ref[:, 0:1]
    for s in range(shards):
        scores = dg(low, queries[s][...], 1, 1) - logs
        high = jnp.max(scores, axis=0, keepdims=True)
        stats_ref[s : s + 1, :] = high
        terms = jnp.exp(scores - high)
        terms_ref[s] = terms
        stats_ref[shards + s : shards + s + 1, :] = jnp.sum(terms, axis=0, keepdims=True)
    stats_ref[2 * shards : 2 * shards + 1, :] = w_ref[...]
    stats_ref[2 * shards + 1 : 2 * shards + 2, :] = pos_ref[...].astype(F32)


def grad_kernel(groups, shards, put_ref, unit_ref, length_ref, terms_ref, *refs):
    queries = refs[:shards]
    stats = refs[shards : 2 * shards]
    summed_ref, lse_ref = refs[2 * shards : 2 * shards + 2]
    outs = refs[2 * shards + 2 :]
    rows = unit_ref.shape[0]
    item = iota((rows, 1), 0) + lax.axis_index("dp") * rows
    total = None
    for u in range(shards):
        highs = [stats[t][(t ^ u) : (t ^ u) + 1, :] for t in range(shards)]
        sums = [stats[t][shards + (t ^ u) : shards + (t ^ u) + 1, :] for t in range(shards)]
        high = functools.reduce(jnp.maximum, highs)
        lse = high + jnp.log(sum(l * jnp.exp(m - high) for l, m in zip(sums, highs)))
        if u == 0:
            lse_ref[...] = lse
        weight = stats[u][2 * shards : 2 * shards + 1, :]
        target = stats[u][2 * shards + 1 : 2 * shards + 2, :].astype(jnp.int32)
        scale = weight * jnp.exp(highs[0] - lse)
        coeff = (terms_ref[u] * scale - jnp.where(item == target, weight, 0.0)).astype(BF)
        part = dg(coeff, queries[u][...], 1, 0)
        total = part if total is None else total + part
    unit = unit_ref[...]
    along = jnp.sum(unit * total, axis=1, keepdims=True)
    summed = (total - unit * along) / length_ref[:, 0:1]
    summed_ref[...] = summed
    low_grad = summed.astype(BF)
    size = outs[0].shape[0]
    for s in range(groups):
        outs[s][...] = dg(put_ref[s * size : (s + 1) * size, :], low_grad, 1, 0).astype(BF)


def turned(row):
    return jnp.transpose(jnp.broadcast_to(row, (128, row.shape[1])))


def query_kernel(shards, query_ref, counts_ref, lse_ref, w_ref, pos_ref, *refs):
    units = refs[:shards]
    loss_ref, grad_ref = refs[shards:]
    rows = units[0].shape[0]
    me = lax.axis_index("dp")
    query = query_ref[...]
    lse, weight = turned(lse_ref[...])[:, 0:1], turned(w_ref[...])[:, 0:1]
    target = turned(pos_ref[...].astype(F32))[:, 0:1].astype(jnp.int32)
    picked, total = None, None
    for u in range(shards):
        shard = lax.bitwise_xor(me, u)
        unit = units[u][...]
        counts = counts_ref[:, pl.ds(pl.multiple_of(shard * rows, 128), rows)]
        scores = dg(query, unit, 1, 1) - jnp.log(counts.astype(F32))
        hit = iota((1, rows), 1) + shard * rows == target
        here = jnp.sum(jnp.where(hit, scores, 0.0), axis=1, keepdims=True)
        coeff = (weight * (jnp.exp(scores - lse) - jnp.where(hit, 1.0, 0.0))).astype(BF)
        part = dg(coeff, unit, 1, 0)
        picked = here if picked is None else picked + here
        total = part if total is None else total + part
    loss = jnp.broadcast_to(lse - picked, (query.shape[0], 128))
    loss_ref[...] = jnp.transpose(loss)[0:1, :]
    grad_ref[...] = total


def backward_kernel(groups, win_ref, wout_ref, slope_ref, *refs):
    gs, outs = refs[:groups], refs[groups:]
    for k in range(win_ref.shape[0]):
        hidden = (dg(expert_rows(gs, k), wout_ref[k], 1, 1) * slope_ref[k]).astype(BF)
        y = dg(hidden, win_ref[k], 1, 1).astype(BF)
        for s in range(groups):
            outs[s][k * CAP : (k + 1) * CAP, :] = y[s * CAP : (s + 1) * CAP, :]


def early_kernel(shards, win_ref, *refs):
    xs = refs[:shards]
    act_ref, slope_ref, xt_ref = refs[shards:]
    me = lax.axis_index("dp")
    win = win_ref[me]
    width = xs[0].shape[0]
    for s in range(shards):
        x = xs[s][...]
        act, slope = gelu_both(dg(win, x, 0, 1))
        act_ref[:, s * width : (s + 1) * width] = act.astype(BF)
        slope_ref[:, s * width : (s + 1) * width] = slope.astype(BF)
        xt_ref[:, s * width : (s + 1) * width] = dg(eye(x.shape[1]), x, 1, 1).astype(BF)


def weight_kernel(shards, wout_ref, act_ref, slope_ref, xt_ref, *refs):
    gs, outs, full = refs[:shards], refs[shards:-1], refs[-1]
    me = lax.axis_index("dp")
    g = jnp.concatenate([r[...] for r in gs], axis=0)
    width = g.shape[1]
    hidden = (dg(wout_ref[me], g, 1, 1) * slope_ref[...].astype(F32)).astype(BF)
    full[...] = dg(xt_ref[...], hidden, 1, 1)
    out_rows, in_rows = act_ref.shape[0] // shards, full.shape[0] // shards
    for s in range(shards):
        peer = lax.bitwise_xor(me, s)
        start = pl.multiple_of(peer * out_rows, out_rows)
        outs[s][:out_rows, :] = dg(act_ref[pl.ds(start, out_rows), :], g, 1, 0).astype(BF)
        start = pl.multiple_of(peer * in_rows, in_rows)
        for c in range(full.shape[1] // width):
            piece = full[pl.ds(start, in_rows), c * width : (c + 1) * width]
            first = out_rows + c * in_rows
            outs[s][first : first + in_rows, :] = piece.astype(BF)


def assemble_kernel(shards, *refs):
    parts, (in_ref, out_ref) = refs[:shards], refs[shards:]
    me = lax.axis_index("dp")
    in_rows, experts, units = in_ref.shape
    out_rows, _, width = out_ref.shape
    size = in_rows * experts
    row, col = iota((size, size), 0), iota((size, size), 1)
    bits = experts.bit_length() - 1
    wanted = lax.bitwise_xor(lax.bitwise_and(row, experts - 1), me) * in_rows
    spread_rows = jnp.where(wanted + lax.shift_right_logical(row, bits) == col, 1.0, 0.0).astype(BF)
    for c in range(units // width):
        first = out_rows + c * in_rows
        stacked = jnp.concatenate([r[first : first + in_rows, :] for r in parts], axis=0)
        block = dg(spread_rows, stacked, 1, 0)
        in_ref[:, :, c * width : (c + 1) * width] = block.reshape(in_rows, experts, width)
    for c in range(out_rows // in_rows):
        first = c * in_rows
        stacked = jnp.concatenate([r[first : first + in_rows, :] for r in parts], axis=0)
        block = dg(spread_rows, stacked, 1, 0)
        out_ref[first : first + in_rows] = block.reshape(in_rows, experts, width)


def final_kernel(groups, feats_ref, pick_ref, summed_ref, *refs):
    blocks, out_ref = refs[:groups], refs[groups]
    x = feats_ref[...].astype(F32)
    r = inv_rms_of(x)
    rows = gather_rows(pick_ref, blocks)
    projected = jnp.mean(rows * x, axis=1, keepdims=True)
    out_ref[...] = summed_ref[...] + r * (rows - x * (r * r) * projected)


def call(body, outs, args, flops=0, touched=0, trans=0, scratch=(), space=pltpu.VMEM):
    shapes = [jax.ShapeDtypeStruct(s, d) for s, d in outs]
    spaces = space if isinstance(space, list) else [space] * len(args)
    return pl.pallas_call(
        body,
        out_shape=shapes,
        in_specs=[pl.BlockSpec(memory_space=m) for m in spaces],
        out_specs=[pl.BlockSpec(memory_space=pltpu.VMEM)] * len(outs),
        scratch_shapes=list(scratch),
        cost_estimate=pl.CostEstimate(flops=flops, bytes_accessed=touched, transcendentals=trans),
        compiler_params=pltpu.CompilerParams(vmem_limit_bytes=24 << 20),
    )(*args)


def shift_by(values, axis, s):
    n = lax.axis_size(axis)
    return lax.ppermute(values, axis, [(i, i ^ s) for i in range(n)])


def exchange(blocks, axis):
    return [blocks[0]] + [shift_by(b, axis, s) for s, b in enumerate(blocks) if s > 0]


def spread(block, axis):
    return exchange([block] * lax.axis_size(axis), axis)


def per_device(
    item_feats, expert_ids, weight_in, weight_out, queries, query_weight, positives, sample_counts
):
    groups, shards = lax.axis_size("expert"), lax.axis_size("dp")
    local_experts, width, units = weight_in.shape
    rows, q_rows = item_feats.shape[1], queries.shape[1]
    experts_all = local_experts * groups
    feats = item_feats[0]
    ids = expert_ids.reshape(1, rows)
    slots = local_experts * CAP
    query = queries[0]
    block = ((slots, width), BF)
    matmul = 2 * rows * q_rows * shards * width
    expert_flops = 2 * groups * slots * width * units

    slot, *packed = call(
        functools.partial(pack_kernel, local_experts, experts_all, groups),
        [((1, rows), jnp.int32)] + [block] * groups,
        [pltpu.with_memory_space_constraint(v, pltpu.HBM) for v in (ids, feats)],
        flops=2 * groups * slots * rows * width,
        touched=1 << 20,
        scratch=[
            pltpu.VMEM((1, rows), jnp.int32),
            pltpu.VMEM((rows, width), BF),
            pltpu.SemaphoreType.DMA(()),
            pltpu.SemaphoreType.DMA(()),
        ],
        space=pltpu.HBM,
    )
    received = exchange(packed, "expert")
    all_queries = spread(query, "dp")
    weight_in, weight_out, pick, put, logs = call(
        load_kernel,
        [
            (weight_in.shape, BF),
            (weight_out.shape, BF),
            ((rows, groups * slots), BF),
            ((groups * slots, rows), BF),
            ((rows, 128), F32),
        ],
        (
            pltpu.with_memory_space_constraint(weight_in, pltpu.HBM),
            pltpu.with_memory_space_constraint(weight_out, pltpu.HBM),
            slot,
            sample_counts,
        ),
        touched=16 << 20,
        scratch=[pltpu.SemaphoreType.DMA(()), pltpu.SemaphoreType.DMA(())],
        space=[pltpu.HBM, pltpu.HBM, pltpu.VMEM, pltpu.VMEM],
    )
    output = call(
        functools.partial(forward_kernel, groups),
        [block] * groups,
        (weight_in, weight_out, *received),
        flops=2 * expert_flops,
        touched=6 << 20,
        trans=groups * slots * units,
    )
    returned = exchange(output, "expert")
    (slope,) = call(
        functools.partial(slope_kernel, groups),
        [((local_experts, groups * CAP, units), F32)],
        (weight_in, *received),
        flops=expert_flops,
        touched=6 << 20,
        trans=groups * slots * units,
    )
    low, unit, length, stats, terms = call(
        functools.partial(unit_kernel, groups, shards),
        [
            ((rows, width), BF),
            ((rows, width), F32),
            ((rows, 128), F32),
            ((2 * shards + 2, q_rows), F32),
            ((shards, rows, q_rows), F32),
        ],
        (feats, pick, logs, query_weight, positives, *returned, *all_queries),
        flops=2 * matmul,
        touched=4 << 20,
        trans=rows * q_rows * shards,
    )
    all_stats = spread(stats, "dp")
    summed, lse, *packed_grads = call(
        functools.partial(grad_kernel, groups, shards),
        [((rows, width), F32), ((1, q_rows), F32)] + [block] * groups,
        (put, unit, length, terms, *all_queries, *all_stats),
        flops=3 * matmul,
        touched=4 << 20,
        trans=rows * q_rows * shards,
    )
    received_grads = exchange(packed_grads, "expert")
    all_units = spread(low, "dp")
    query_loss, grad_queries = call(
        functools.partial(query_kernel, shards),
        [((1, q_rows), F32), ((q_rows, width), F32)],
        (query, sample_counts, lse, query_weight, positives, *all_units),
        flops=2 * matmul,
        touched=3 << 20,
        trans=rows * q_rows * shards,
    )
    grad_out = call(
        functools.partial(backward_kernel, groups),
        [block] * groups,
        (weight_in, weight_out, slope, *received_grads),
        flops=2 * expert_flops,
        touched=6 << 20,
        trans=groups * slots * units,
    )
    grad_back = exchange(grad_out, "expert")
    (grad_items,) = call(
        functools.partial(final_kernel, groups),
        [((rows, width), F32)],
        (feats, pick, summed, *grad_back),
        flops=2 * groups * slots * rows * width,
        touched=2 << 20,
    )
    if shards == local_experts:
        tokens = ((groups * CAP, width), BF)
        regroup = functools.partial(regroup_kernel, groups, shards)
        own_x = exchange(call(regroup, [tokens] * shards, received, touched=1 << 20), "dp")
        total_rows = shards * groups * CAP
        act, act_slope, xt = call(
            functools.partial(early_kernel, shards),
            [((units, total_rows), BF), ((units, total_rows), BF), ((width, total_rows), BF)],
            (weight_in, *own_x),
            flops=expert_flops,
            touched=6 << 20,
            trans=total_rows * units,
        )
        own_g = exchange(call(regroup, [tokens] * shards, received_grads, touched=1 << 20), "dp")
        parts = exchange(
            call(
                functools.partial(weight_kernel, shards),
                [((units // shards + units // shards, width), BF)] * shards,
                (weight_out, act, act_slope, xt, *own_g),
                flops=3 * expert_flops,
                touched=6 << 20,
                scratch=[pltpu.VMEM((width, units), F32)],
            ),
            "dp",
        )
        grad_weight_in, grad_weight_out = call(
            functools.partial(assemble_kernel, shards),
            [
                ((width // shards, local_experts, units), F32),
                ((units // shards, local_experts, width), F32),
            ],
            parts,
            flops=expert_flops,
            touched=6 << 20,
        )
    else:
        x = jnp.stack(received).reshape(groups, local_experts, CAP, width)
        g = jnp.stack(received_grads).reshape(groups, local_experts, CAP, width)
        hidden = jnp.einsum("skcd,kdf->skcf", x, weight_in, preferred_element_type=F32)
        active, slope = gelu_both(hidden)
        grad_active = jnp.einsum("skcd,kfd->skcf", g, weight_out, preferred_element_type=F32)
        grad_hidden = (grad_active * slope).astype(BF)

        def reduce(a, b):
            part = jnp.einsum("skcr,skcf->rkf", a, b, preferred_element_type=F32).astype(BF)
            return lax.psum_scatter(part, "dp", scatter_dimension=0, tiled=True).astype(F32)

        grad_weight_in, grad_weight_out = reduce(x, grad_hidden), reduce(active.astype(BF), g)
    return (query_loss, grad_queries[None], grad_items[None], grad_weight_in, grad_weight_out)


def solution(mesh):
    placed = (
        P("expert", "dp", None),
        P("expert", "dp", None),
        P("expert", None, None),
        P("expert", None, None),
        P("expert", "dp", None),
        P("expert", "dp"),
        P("expert", "dp"),
        P("expert", None),
    )

    return jax.shard_map(
        per_device,
        mesh=mesh,
        in_specs=placed,
        out_specs=(
            P("expert", "dp"),
            P("expert", "dp", None),
            P("expert", "dp", None),
            P("dp", "expert", None),
            P("dp", "expert", None),
        ),
        check_vma=False,
    )
```

```python
import functools

import jax
import jax.numpy as jnp
from jax import lax
from jax.experimental import pallas as pl
from jax.experimental.pallas import tpu as pltpu
from jax.sharding import PartitionSpec as P

CAP = 32
CUT = 256
norm_eps = 1e-06
BF = jnp.bfloat16
F32 = jnp.float32
GELU_C = 0.7978845608028654
GELU_A = 0.044715


def dg(a, b, ca, cb):
    return lax.dot_general(a, b, (((ca,), (cb,)), ((), ())), preferred_element_type=F32)


def iota(shape, axis):
    return lax.broadcasted_iota(jnp.int32, shape, axis)


def eye(n):
    return jnp.where(iota((n, n), 0) == iota((n, n), 1), 1.0, 0.0).astype(BF)


def to_col(row):
    n = row.shape[1]
    sub = iota((16, n), 0)
    high = lax.shift_right_logical(row, 8)
    low = lax.bitwise_and(row, 255)
    halves = jnp.where(sub == 0, high, jnp.where(sub == 1, low, 0)).astype(F32).astype(BF)
    cols = dg(eye(n), halves, 1, 1)
    return cols[:, 0:1] * 256.0 + cols[:, 1:2]


def gelu(v):
    half = 0.5 * v
    return half + half * jnp.tanh(v * (GELU_C + (GELU_A * GELU_C) * (v * v)))


def gelu_both(v):
    sq = v * v
    th = jnp.tanh(v * (GELU_C + (GELU_A * GELU_C) * sq))
    half = 0.5 * (1.0 + th)
    slope = half + 0.5 * v * (1.0 - th * th) * (GELU_C + (3.0 * GELU_A * GELU_C) * sq)
    return v * half, slope


def scatter_matrix(slot_row, block, rows):
    return jnp.where(iota((rows, slot_row.shape[1]), 0) + block * rows == slot_row, 1.0, 0.0).astype(BF)


def gather_rows(pick_ref, blocks):
    return dg(pick_ref[...], jnp.concatenate([b[...] for b in blocks], axis=0), 1, 0)


def put_row(ref, index, row):
    pieces = row.shape[1] // 128
    for c in range(pieces):
        ref[index * pieces + c : index * pieces + c + 1, :] = row[:, c * 128 : (c + 1) * 128]


def get_row(ref, index, width):
    pieces = width // 128
    return jnp.concatenate([ref[index * pieces + c : index * pieces + c + 1, :] for c in range(pieces)], axis=1)


def inv_rms_of(x):
    return lax.rsqrt(jnp.mean(x * x, axis=1, keepdims=True) + norm_eps)


def pack_kernel(local_experts, experts_all, groups, ids_hbm, feats_hbm, *refs):
    slot_ref, blocks = refs[0], refs[1 : groups + 1]
    ids_ref, feats_ref, ids_sem, feats_sem = refs[groups + 1 :]
    ids_copy = pltpu.make_async_copy(ids_hbm, ids_ref, ids_sem)
    feats_copy = pltpu.make_async_copy(feats_hbm, feats_ref, feats_sem)
    ids_copy.start()
    feats_copy.start()
    me = lax.axis_index("expert")
    ids_copy.wait()
    ids = ids_ref[...]
    n = ids.shape[1]
    shift = local_experts.bit_length() - 1
    hot = iota((experts_all, n), 0) == ids
    tri = jnp.where(iota((n, n), 0) < iota((n, n), 1), 1.0, 0.0).astype(BF)
    before = dg(jnp.where(hot, 1.0, 0.0).astype(BF), tri, 1, 0)
    rank = jnp.sum(jnp.where(hot, before, 0.0), axis=0, keepdims=True).astype(jnp.int32)
    owner = lax.bitwise_xor(lax.shift_right_logical(ids, shift), me)
    local = lax.bitwise_and(ids, local_experts - 1)
    slot = (owner * local_experts + local) * CAP + rank
    slot_ref[...] = slot
    feats_copy.wait()
    x = feats_ref[...].astype(F32)
    normed = (x * inv_rms_of(x)).astype(BF)
    rows = local_experts * CAP
    for s in range(groups):
        blocks[s][...] = dg(scatter_matrix(slot, s, rows), normed, 1, 0).astype(BF)


def load_kernel(
    win_hbm, wout_hbm, slot_ref, counts_ref, win_ref, wout_ref, pick_ref, put_ref, logs_ref, in_sem, out_sem
):
    copies = (
        pltpu.make_async_copy(win_hbm, win_ref, in_sem),
        pltpu.make_async_copy(wout_hbm, wout_ref, out_sem),
    )
    for copy in copies:
        copy.start()
    slot = slot_ref[...]
    col = to_col(slot).astype(jnp.int32)
    pick_ref[...] = jnp.where(iota(pick_ref.shape, 1) == col, 1.0, 0.0).astype(BF)
    put_ref[...] = scatter_matrix(slot, 0, put_ref.shape[0])
    logs = log_counts_col(counts_ref, lax.axis_index("dp"), slot.shape[1])
    logs_ref[...] = jnp.broadcast_to(logs, logs_ref.shape)
    for copy in copies:
        copy.wait()


def expert_rows(blocks, k):
    return jnp.concatenate([b[k * CAP : (k + 1) * CAP, :] for b in blocks], axis=0)


def forward_kernel(groups, win_ref, wout_ref, *refs):
    blocks, outs = refs[:groups], refs[groups:]
    for k in range(win_ref.shape[0]):
        x = expert_rows(blocks, k)
        act = gelu(dg(x, win_ref[k], 1, 0)).astype(BF)
        y = dg(act, wout_ref[k], 1, 0).astype(BF)
        for s in range(groups):
            outs[s][k * CAP : (k + 1) * CAP, :] = y[s * CAP : (s + 1) * CAP, :]


def slope_kernel(groups, win_ref, *refs):
    blocks, slope_ref = refs[:groups], refs[groups]
    for k in range(win_ref.shape[0]):
        _, slope = gelu_both(dg(expert_rows(blocks, k), win_ref[k], 1, 0))
        slope_ref[k] = slope


def regroup_kernel(groups, shards, *refs):
    blocks, outs = refs[:groups], refs[groups:]
    me = lax.axis_index("dp")
    for s in range(shards):
        start = pl.multiple_of(lax.bitwise_xor(me, s) * CAP, CAP)
        for g in range(groups):
            outs[s][g * CAP : (g + 1) * CAP, :] = blocks[g][pl.ds(start, CAP), :]


def log_counts_col(counts_ref, shard, rows):
    part = counts_ref[:, pl.ds(pl.multiple_of(shard * rows, 128), rows)]
    return jnp.log(to_col(part))


def unit_kernel(groups, shards, feats_ref, pick_ref, logs_ref, w_ref, pos_ref, *refs):
    blocks = refs[:groups]
    queries = refs[groups : groups + shards]
    low_ref, unit_ref, length_ref, stats_ref, terms_ref = refs[groups + shards :]
    branch = gather_rows(pick_ref, blocks)
    summed = feats_ref[...].astype(F32) + branch
    length = jnp.sqrt(jnp.sum(summed * summed, axis=1, keepdims=True) + norm_eps)
    unit = summed / length
    low = unit.astype(BF)
    low_ref[...] = low
    unit_ref[...] = unit
    length_ref[...] = jnp.broadcast_to(length, length_ref.shape)
    logs = logs_ref[:, 0:1]
    cuts = [slice(i, i + CUT) for i in range(0, low.shape[0], CUT)]
    for s in range(shards):
        high, total = None, None
        for cut in cuts:
            scores = dg(low[cut], queries[s][...], 1, 1) - logs[cut]
            terms_ref[s, cut, :] = scores
            top = jnp.max(scores, axis=0, keepdims=True)
            high = top if high is None else jnp.maximum(high, top)
        put_row(stats_ref, s, high)
        for cut in cuts:
            terms = jnp.exp(terms_ref[s, cut, :] - high)
            terms_ref[s, cut, :] = terms
            part = jnp.sum(terms, axis=0, keepdims=True)
            total = part if total is None else total + part
        put_row(stats_ref, shards + s, total)
    put_row(stats_ref, 2 * shards, w_ref[...])
    put_row(stats_ref, 2 * shards + 1, pos_ref[...].astype(F32))


def grad_kernel(groups, shards, put_ref, unit_ref, length_ref, terms_ref, *refs):
    queries = refs[:shards]
    stats = refs[shards : 2 * shards]
    summed_ref, lse_ref = refs[2 * shards : 2 * shards + 2]
    outs = refs[2 * shards + 2 :]
    rows, q_rows = unit_ref.shape[0], terms_ref.shape[2]
    item = iota((rows, 1), 0) + lax.axis_index("dp") * rows
    total = None
    for u in range(shards):
        highs = [get_row(stats[t], t ^ u, q_rows) for t in range(shards)]
        sums = [get_row(stats[t], shards + (t ^ u), q_rows) for t in range(shards)]
        high = functools.reduce(jnp.maximum, highs)
        lse = high + jnp.log(sum(l * jnp.exp(m - high) for l, m in zip(sums, highs)))
        if u == 0:
            lse_ref[...] = lse
        weight = get_row(stats[u], 2 * shards, q_rows)
        target = get_row(stats[u], 2 * shards + 1, q_rows).astype(jnp.int32)
        scale = weight * jnp.exp(highs[0] - lse)
        coeff = (terms_ref[u] * scale - jnp.where(item == target, weight, 0.0)).astype(BF)
        part = dg(coeff, queries[u][...], 1, 0)
        total = part if total is None else total + part
    unit = unit_ref[...]
    along = jnp.sum(unit * total, axis=1, keepdims=True)
    summed = (total - unit * along) / length_ref[:, 0:1]
    summed_ref[...] = summed
    low_grad = summed.astype(BF)
    size = outs[0].shape[0]
    for s in range(groups):
        outs[s][...] = dg(put_ref[s * size : (s + 1) * size, :], low_grad, 1, 0).astype(BF)


def turned(row):
    return jnp.transpose(jnp.broadcast_to(row, (128, row.shape[1])))


def query_kernel(shards, query_ref, counts_ref, lse_ref, w_ref, pos_ref, *refs):
    units = refs[:shards]
    loss_ref, grad_ref = refs[shards:]
    rows = units[0].shape[0]
    me = lax.axis_index("dp")
    query = query_ref[...]
    lse, weight = turned(lse_ref[...])[:, 0:1], turned(w_ref[...])[:, 0:1]
    target = turned(pos_ref[...].astype(F32))[:, 0:1].astype(jnp.int32)
    picked, total = None, None
    for u in range(shards):
        shard = lax.bitwise_xor(me, u)
        unit = units[u][...]
        counts = counts_ref[:, pl.ds(pl.multiple_of(shard * rows, 128), rows)]
        scores = dg(query, unit, 1, 1) - jnp.log(counts.astype(F32))
        hit = iota((1, rows), 1) + shard * rows == target
        here = jnp.sum(jnp.where(hit, scores, 0.0), axis=1, keepdims=True)
        coeff = (weight * (jnp.exp(scores - lse) - jnp.where(hit, 1.0, 0.0))).astype(BF)
        part = dg(coeff, unit, 1, 0)
        picked = here if picked is None else picked + here
        total = part if total is None else total + part
    loss = jnp.broadcast_to(lse - picked, (query.shape[0], 128))
    loss_ref[...] = jnp.transpose(loss)[0:1, :]
    grad_ref[...] = total


def backward_kernel(groups, win_ref, wout_ref, slope_ref, *refs):
    gs, outs = refs[:groups], refs[groups:]
    for k in range(win_ref.shape[0]):
        hidden = (dg(expert_rows(gs, k), wout_ref[k], 1, 1) * slope_ref[k]).astype(BF)
        y = dg(hidden, win_ref[k], 1, 1).astype(BF)
        for s in range(groups):
            outs[s][k * CAP : (k + 1) * CAP, :] = y[s * CAP : (s + 1) * CAP, :]


def early_kernel(shards, win_ref, *refs):
    xs = refs[:shards]
    act_ref, slope_ref, xt_ref = refs[shards:]
    me = lax.axis_index("dp")
    win = win_ref[me]
    width = xs[0].shape[0]
    for s in range(shards):
        x = xs[s][...]
        act, slope = gelu_both(dg(win, x, 0, 1))
        act_ref[:, s * width : (s + 1) * width] = act.astype(BF)
        slope_ref[:, s * width : (s + 1) * width] = slope.astype(BF)
        xt_ref[:, s * width : (s + 1) * width] = dg(eye(x.shape[1]), x, 1, 1).astype(BF)


def weight_kernel(shards, wout_ref, act_ref, slope_ref, xt_ref, *refs):
    gs, outs, full = refs[:shards], refs[shards:-1], refs[-1]
    me = lax.axis_index("dp")
    g = jnp.concatenate([r[...] for r in gs], axis=0)
    width = g.shape[1]
    hidden = (dg(wout_ref[me], g, 1, 1) * slope_ref[...].astype(F32)).astype(BF)
    full[...] = dg(xt_ref[...], hidden, 1, 1)
    out_rows, in_rows = act_ref.shape[0] // shards, full.shape[0] // shards
    for s in range(shards):
        peer = lax.bitwise_xor(me, s)
        start = pl.multiple_of(peer * out_rows, out_rows)
        outs[s][:out_rows, :] = dg(act_ref[pl.ds(start, out_rows), :], g, 1, 0).astype(BF)
        start = pl.multiple_of(peer * in_rows, in_rows)
        for c in range(full.shape[1] // width):
            piece = full[pl.ds(start, in_rows), c * width : (c + 1) * width]
            first = out_rows + c * in_rows
            outs[s][first : first + in_rows, :] = piece.astype(BF)


def assemble_kernel(shards, *refs):
    parts, (in_ref, out_ref) = refs[:shards], refs[shards:]
    me = lax.axis_index("dp")
    in_rows, experts, units = in_ref.shape
    out_rows, _, width = out_ref.shape
    size = in_rows * experts
    row, col = iota((size, size), 0), iota((size, size), 1)
    bits = experts.bit_length() - 1
    wanted = lax.bitwise_xor(lax.bitwise_and(row, experts - 1), me) * in_rows
    spread_rows = jnp.where(wanted + lax.shift_right_logical(row, bits) == col, 1.0, 0.0).astype(BF)
    for c in range(units // width):
        first = out_rows + c * in_rows
        stacked = jnp.concatenate([r[first : first + in_rows, :] for r in parts], axis=0)
        block = dg(spread_rows, stacked, 1, 0)
        in_ref[:, :, c * width : (c + 1) * width] = block.reshape(in_rows, experts, width)
    for c in range(out_rows // in_rows):
        first = c * in_rows
        stacked = jnp.concatenate([r[first : first + in_rows, :] for r in parts], axis=0)
        block = dg(spread_rows, stacked, 1, 0)
        out_ref[first : first + in_rows] = block.reshape(in_rows, experts, width)


def final_kernel(groups, feats_ref, pick_ref, summed_ref, *refs):
    blocks, out_ref = refs[:groups], refs[groups]
    x = feats_ref[...].astype(F32)
    r = inv_rms_of(x)
    rows = gather_rows(pick_ref, blocks)
    projected = jnp.mean(rows * x, axis=1, keepdims=True)
    out_ref[...] = summed_ref[...] + r * (rows - x * (r * r) * projected)


def call(body, outs, args, flops=0, touched=0, trans=0, scratch=(), space=pltpu.VMEM):
    shapes = [jax.ShapeDtypeStruct(s, d) for s, d in outs]
    spaces = space if isinstance(space, list) else [space] * len(args)
    return pl.pallas_call(
        body,
        out_shape=shapes,
        in_specs=[pl.BlockSpec(memory_space=m) for m in spaces],
        out_specs=[pl.BlockSpec(memory_space=pltpu.VMEM)] * len(outs),
        scratch_shapes=list(scratch),
        cost_estimate=pl.CostEstimate(flops=flops, bytes_accessed=touched, transcendentals=trans),
        compiler_params=pltpu.CompilerParams(vmem_limit_bytes=24 << 20),
    )(*args)


def shift_by(values, axis, s):
    n = lax.axis_size(axis)
    return lax.ppermute(values, axis, [(i, i ^ s) for i in range(n)])


def exchange(blocks, axis):
    return [blocks[0]] + [shift_by(b, axis, s) for s, b in enumerate(blocks) if s > 0]


def spread(block, axis):
    return exchange([block] * lax.axis_size(axis), axis)


def per_device(
    item_feats, expert_ids, weight_in, weight_out, queries, query_weight, positives, sample_counts
):
    groups, shards = lax.axis_size("expert"), lax.axis_size("dp")
    local_experts, width, units = weight_in.shape
    rows, q_rows = item_feats.shape[1], queries.shape[1]
    experts_all = local_experts * groups
    feats = item_feats[0]
    ids = expert_ids.reshape(1, rows)
    slots = local_experts * CAP
    query = queries[0]
    block = ((slots, width), BF)
    matmul = 2 * rows * q_rows * shards * width
    expert_flops = 2 * groups * slots * width * units

    slot, *packed = call(
        functools.partial(pack_kernel, local_experts, experts_all, groups),
        [((1, rows), jnp.int32)] + [block] * groups,
        [pltpu.with_memory_space_constraint(v, pltpu.HBM) for v in (ids, feats)],
        flops=2 * groups * slots * rows * width,
        touched=1 << 20,
        scratch=[
            pltpu.VMEM((1, rows), jnp.int32),
            pltpu.VMEM((rows, width), BF),
            pltpu.SemaphoreType.DMA(()),
            pltpu.SemaphoreType.DMA(()),
        ],
        space=pltpu.HBM,
    )
    received = exchange(packed, "expert")
    all_queries = spread(query, "dp")
    weight_in, weight_out, pick, put, logs = call(
        load_kernel,
        [
            (weight_in.shape, BF),
            (weight_out.shape, BF),
            ((rows, groups * slots), BF),
            ((groups * slots, rows), BF),
            ((rows, 128), F32),
        ],
        (
            pltpu.with_memory_space_constraint(weight_in, pltpu.HBM),
            pltpu.with_memory_space_constraint(weight_out, pltpu.HBM),
            slot,
            sample_counts,
        ),
        touched=16 << 20,
        scratch=[pltpu.SemaphoreType.DMA(()), pltpu.SemaphoreType.DMA(())],
        space=[pltpu.HBM, pltpu.HBM, pltpu.VMEM, pltpu.VMEM],
    )
    output = call(
        functools.partial(forward_kernel, groups),
        [block] * groups,
        (weight_in, weight_out, *received),
        flops=2 * expert_flops,
        touched=6 << 20,
        trans=groups * slots * units,
    )
    returned = exchange(output, "expert")
    (slope,) = call(
        functools.partial(slope_kernel, groups),
        [((local_experts, groups * CAP, units), F32)],
        (weight_in, *received),
        flops=expert_flops,
        touched=6 << 20,
        trans=groups * slots * units,
    )
    low, unit, length, stats, terms = call(
        functools.partial(unit_kernel, groups, shards),
        [
            ((rows, width), BF),
            ((rows, width), F32),
            ((rows, 128), F32),
            (((2 * shards + 2) * q_rows // 128, 128), F32),
            ((shards, rows, q_rows), F32),
        ],
        (feats, pick, logs, query_weight, positives, *returned, *all_queries),
        flops=2 * matmul,
        touched=4 << 20,
        trans=rows * q_rows * shards,
    )
    all_stats = spread(stats, "dp")
    summed, lse, *packed_grads = call(
        functools.partial(grad_kernel, groups, shards),
        [((rows, width), F32), ((1, q_rows), F32)] + [block] * groups,
        (put, unit, length, terms, *all_queries, *all_stats),
        flops=3 * matmul,
        touched=4 << 20,
        trans=rows * q_rows * shards,
    )
    received_grads = exchange(packed_grads, "expert")
    all_units = spread(low, "dp")
    query_loss, grad_queries = call(
        functools.partial(query_kernel, shards),
        [((1, q_rows), F32), ((q_rows, width), F32)],
        (query, sample_counts, lse, query_weight, positives, *all_units),
        flops=2 * matmul,
        touched=3 << 20,
        trans=rows * q_rows * shards,
    )
    grad_out = call(
        functools.partial(backward_kernel, groups),
        [block] * groups,
        (weight_in, weight_out, slope, *received_grads),
        flops=2 * expert_flops,
        touched=6 << 20,
        trans=groups * slots * units,
    )
    grad_back = exchange(grad_out, "expert")
    (grad_items,) = call(
        functools.partial(final_kernel, groups),
        [((rows, width), F32)],
        (feats, pick, summed, *grad_back),
        flops=2 * groups * slots * rows * width,
        touched=2 << 20,
    )
    if shards == local_experts:
        tokens = ((groups * CAP, width), BF)
        regroup = functools.partial(regroup_kernel, groups, shards)
        own_x = exchange(call(regroup, [tokens] * shards, received, touched=1 << 20), "dp")
        total_rows = shards * groups * CAP
        act, act_slope, xt = call(
            functools.partial(early_kernel, shards),
            [((units, total_rows), BF), ((units, total_rows), BF), ((width, total_rows), BF)],
            (weight_in, *own_x),
            flops=expert_flops,
            touched=6 << 20,
            trans=total_rows * units,
        )
        own_g = exchange(call(regroup, [tokens] * shards, received_grads, touched=1 << 20), "dp")
        parts = exchange(
            call(
                functools.partial(weight_kernel, shards),
                [((units // shards + units // shards, width), BF)] * shards,
                (weight_out, act, act_slope, xt, *own_g),
                flops=3 * expert_flops,
                touched=6 << 20,
                scratch=[pltpu.VMEM((width, units), F32)],
            ),
            "dp",
        )
        grad_weight_in, grad_weight_out = call(
            functools.partial(assemble_kernel, shards),
            [
                ((width // shards, local_experts, units), F32),
                ((units // shards, local_experts, width), F32),
            ],
            parts,
            flops=expert_flops,
            touched=6 << 20,
        )
    else:
        x = jnp.stack(received).reshape(groups, local_experts, CAP, width)
        g = jnp.stack(received_grads).reshape(groups, local_experts, CAP, width)
        hidden = jnp.einsum("skcd,kdf->skcf", x, weight_in, preferred_element_type=F32)
        active, slope = gelu_both(hidden)
        grad_active = jnp.einsum("skcd,kfd->skcf", g, weight_out, preferred_element_type=F32)
        grad_hidden = (grad_active * slope).astype(BF)

        def reduce(a, b):
            part = jnp.einsum("skcr,skcf->rkf", a, b, preferred_element_type=F32).astype(BF)
            return lax.psum_scatter(part, "dp", scatter_dimension=0, tiled=True).astype(F32)

        grad_weight_in, grad_weight_out = reduce(x, grad_hidden), reduce(active.astype(BF), g)
    return (query_loss, grad_queries[None], grad_items[None], grad_weight_in, grad_weight_out)


def solution(mesh):
    placed = (
        P("expert", "dp", None),
        P("expert", "dp", None),
        P("expert", None, None),
        P("expert", None, None),
        P("expert", "dp", None),
        P("expert", "dp"),
        P("expert", "dp"),
        P("expert", None),
    )

    return jax.shard_map(
        per_device,
        mesh=mesh,
        in_specs=placed,
        out_specs=(
            P("expert", "dp"),
            P("expert", "dp", None),
            P("expert", "dp", None),
            P("dp", "expert", None),
            P("dp", "expert", None),
        ),
        check_vma=False,
    )
```
